128 devices in a mesh: aux: 4 (over y_lo, core), pair: 32 (over z, y_hi, x).
Axes of the slice: x: 4, y: 4 (y_hi: 2, y_lo: 2; y = y_hi * 2 + y_lo), z: 4, core: 2. Of those that a mesh axis runs over, the one named last changes fastest.
Arguments:
- amplitudes: bfloat16 [65536, 512], P('pair', 'aux'), may hold values from -4 to 4
- coulomb: bfloat16 [65536, 512], P('pair'), may hold values from -12 to 12
- df_factors: bfloat16 [65536, 2048], P('pair', 'aux'), may hold values from -0.07861328 to 0.07861328
- thc_left: bfloat16 [512, 1536], P('pair', 'aux'), may hold values from -0.50390625 to 0.50390625
- thc_right: bfloat16 [512, 1536], P('pair', 'aux'), may hold values from -0.50390625 to 0.50390625
- occ_energy: float32 [128], P('pair'), may hold values from -2 to -0.5
- vir_energy: float32 [512], replicated, may hold values from 0.5 to 3
- pivot_energy: float32 [1], replicated, may hold values from -2 to -0.5
Outputs:
- updated: bfloat16 [65536, 512], P('pair', 'aux')
The draws below stay inside these ranges and needn't reach their ends.
All inputs are finite; a program needn't handle non-finite values.
Results may differ from the reference program's by a relative error of at most 0.0051.
Values may be sent and summed in bfloat16 or wider, within the bound.
A program may use at most 64 MiB of HBM per device.

```python
import jax
import jax.numpy as jnp
from jax import lax

V = 512
NAUX = 2048
NTHC = 1536
ITERS = 2
OCC = 128
PAIRS = 65536
N_AUX = 4


def block_levels(rng, dims, cuts, smallest, high):
    factor_of, own = 1.0, jax.random.fold_in(rng, 6)
    for axis_at, parts in cuts:
        steps = jnp.exp(jax.random.uniform(jax.random.fold_in(own, axis_at), (parts,), jnp.float32, smallest / len(cuts), high / len(cuts)))
        factor_of = factor_of * jnp.repeat(steps, dims[axis_at] // parts).reshape([-1 if axis == axis_at else 1 for axis in range(len(dims))])
    return factor_of


def centred(own_key, shape, deviation, limit, pieces=(), held_as=jnp.bfloat16):
    gain = block_levels(own_key, shape, pieces, -0.22, 0.18) if pieces else 1.0
    entries = jax.random.normal(own_key, shape, jnp.float32) * deviation * gain
    return jnp.minimum(jnp.maximum(entries, -limit), limit).astype(held_as)


def setup_inputs(seed: int = 0) -> dict:
    key_of = jax.random.split(jax.random.key(seed), 9)
    amplitudes = centred(key_of[0], (PAIRS, V), 0.5, 4.0, ((0, 32), (1, 4)))
    coulomb = centred(key_of[1], (PAIRS, V), 2.0, 12.0, ((0, 32),))
    df_factors = centred(key_of[2], (PAIRS, NAUX), ((2.0 / (NAUX * PAIRS) ** 0.5) ** 0.5), 0.07861328, ((0, 32), (1, 4)))
    thc_left = centred(key_of[3], (V, NTHC), ((V * NTHC ** 0.5) ** -0.25), 0.50390625, ((0, 32), (1, 4)))
    thc_right = centred(key_of[4], (V, NTHC), ((V * NTHC ** 0.5) ** -0.25), 0.50390625, ((0, 32), (1, 4)))
    occ_energy = jnp.clip(-2.0 + 1.5 * jax.random.uniform(key_of[5], (OCC,), jnp.float32) ** block_levels(key_of[5], (OCC,), ((0, 32),), -0.2, 0.2), -2.0, -0.5)
    vir_energy = jnp.clip(jax.random.uniform(key_of[6], (V,), jnp.float32, 0.5, 3.0), 0.5, 3.0)
    pivot_energy = jnp.clip(jax.random.uniform(key_of[7], (1,), jnp.float32, -2.0, -0.5), -2.0, -0.5)
    return dict(amplitudes=amplitudes, coulomb=coulomb, df_factors=df_factors, thc_left=thc_left, thc_right=thc_right, occ_energy=occ_energy, vir_energy=vir_energy, pivot_energy=pivot_energy)


def reference(amplitudes, coulomb, df_factors, thc_left, thc_right, occ_energy, vir_energy, pivot_energy):
    denom = (vir_energy[None, :, None] + vir_energy[None, None, :] - occ_energy[:, None, None] - pivot_energy[0]).reshape(PAIRS, V)
    aux_block = NAUX // N_AUX
    rank_block = NTHC // N_AUX
    amps = amplitudes
    for step in range(ITERS):
        total = jnp.zeros((PAIRS, V), jnp.float32)
        for block in range(N_AUX):
            factor_k = df_factors[:, block * aux_block:(block + 1) * aux_block]
            gram = lax.dot_general(factor_k, amps, (((0,), (0,)), ((), ())), preferred_element_type=jnp.float32).astype(jnp.bfloat16)
            cycle = jnp.dot(factor_k, gram, preferred_element_type=jnp.float32)
            left_k = thc_left[:, block * rank_block:(block + 1) * rank_block]
            right_k = thc_right[:, block * rank_block:(block + 1) * rank_block]
            proj = jnp.dot(amps, right_k, preferred_element_type=jnp.float32).reshape(OCC, V, rank_block)
            middle = jnp.sum(proj * left_k.astype(jnp.float32)[None], axis=1)
            weighted = (left_k.astype(jnp.float32)[None] * middle[:, None, :]).astype(jnp.bfloat16).reshape(PAIRS, rank_block)
            ladder = lax.dot_general(weighted, right_k, (((1,), (1,)), ((), ())), preferred_element_type=jnp.float32)
            total = total + (cycle + ladder)
        amps = ((coulomb.astype(jnp.float32) + total) / denom).astype(jnp.bfloat16)
    return amps
```

```python
import jax
import jax.numpy as jnp
from jax import lax
from jax.experimental import pallas as pl
from jax.experimental.pallas import tpu as pltpu
from jax.sharding import PartitionSpec as P

MESH = pl.DeviceIdType.MESH
BF = jnp.bfloat16
F32 = jnp.float32
N_SEM = 256
N_CHUNK = 8
TN = (((0,), (0,)), ((), ()))
NT = (((1,), (1,)), ((), ()))


def kernel(
    amps, coul, df, tl, tr, occ, vir, piv, out,
    BQ, BR, T0, T1, TS, C, LAD, VA, WB, MID,
    GP1, RA1, CB1, RB1, PB1, RY1, G1,
    GP2, RA2, CB2, RB2, PB2, RY2, G2,
    ss, rs, ls,
):
    a = lax.axis_index("aux")
    p = lax.axis_index("pair")
    Y, c = a // 2, a % 2
    z, yh, x = p // 8, (p // 4) % 2, p % 4
    oY, oc, oyh = 1 - Y, 1 - c, 1 - yh

    def dev(Y=Y, c=c, z=z, yh=yh, x=x):
        return {"aux": Y * 2 + c, "pair": z * 8 + yh * 4 + x}

    ypeers = [dev(Y=oY), dev(yh=oyh), dev(Y=oY, yh=oyh)]
    xpeers = [dev(x=(x + k) % 4) for k in (1, 2, 3)]
    zpeers = [dev(z=(z + k) % 4) for k in (1, 2, 3)]
    core = dev(c=oc)
    rows = pl.multiple_of(Y * 1024, 1024)
    orows = pl.multiple_of(oY * 1024, 1024)

    count = [0]
    started = []

    def send(src, dst, to):
        n = count[0]
        count[0] += 1
        assert n < N_SEM
        copy = pltpu.make_async_remote_copy(
            src_ref=src, dst_ref=dst, send_sem=ss.at[n], recv_sem=rs.at[n],
            device_id=to, device_id_type=MESH,
        )
        copy.start()
        started.append(copy)
        return copy

    def arrive(copies):
        for copy in copies:
            copy.wait_recv()

    locals_ = [
        (df, BQ.at[c]),
        (amps, T0.at[Y]),
        (tl, WB.at[c, Y, 0, z, yh, x]),
        (tr, WB.at[c, Y, 1, z, yh, x]),
        (coul.at[pl.ds(rows, 1024), pl.ds(pl.multiple_of(c * 128, 128), 128)], C.at[0]),
        (coul.at[pl.ds(rows, 1024), pl.ds(pl.multiple_of((2 + c) * 128, 128), 128)], C.at[1]),
    ]
    lcopies = []
    for n, (src, dst) in enumerate(locals_):
        copy = pltpu.make_async_copy(src, dst, ls.at[n])
        copy.start()
        lcopies.append(copy)

    barrier = pltpu.get_barrier_semaphore()
    for to in ypeers + xpeers + zpeers + [core]:
        pl.semaphore_signal(barrier, inc=1, device_id=to, device_id_type=MESH)
    pl.semaphore_wait(barrier, 10)

    thc_y = []
    for to in ypeers:
        thc_y.append(send(tl, WB.at[c, Y, 0, z, yh, x], to))
        thc_y.append(send(tr, WB.at[c, Y, 1, z, yh, x], to))
    t_in = send(amps, T0.at[Y], ypeers[0])
    b_in = send(df, BQ.at[c], core)
    size = 1024 // N_CHUNK

    def move(n):
        return send(
            df.at[pl.ds(pl.multiple_of(oY * 1024 + n * size, size), size), :],
            BR.at[c, pl.ds(n * size, size), :],
            ypeers[0],
        )

    def forward(n):
        block = BR.at[c, pl.ds(n * size, size), :]
        return send(block, block, core)

    moved = [move(n) for n in range(N_CHUNK // 2)]

    def gram_tiles(get, tsrc, put):
        def body(q, _):
            qs = pl.multiple_of(q * 256, 256)
            put(qs, lax.dot_general(get(qs), tsrc, TN, preferred_element_type=F32).astype(BF))
            return 0

        lax.fori_loop(0, 2, body, 0)

    def gram1(f, s, cc):
        def get(qs):
            return BQ[cc, :, pl.ds(qs, 256)]

        def put(qs, value):
            GP1[f, 0, pl.ds(pl.multiple_of(cc * 512 + qs, 256), 256), :] = value

        gram_tiles(get, T0[s], put)

    def gram2(s):
        for cc in range(2):
            def put_own(qs, value):
                GP2[s, Y, pl.ds(pl.multiple_of(cc * 512 + qs, 256), 256), :] = value

            def put_other(qs, value):
                GP2[s, oY, pl.ds(pl.multiple_of(cc * 512 + qs, 256), 256), :] = value

            gram_tiles(lambda qs: BQ[cc, pl.ds(rows, 1024), pl.ds(qs, 256)], T1[s], put_own)
            gram_tiles(lambda qs: BR[cc, :, pl.ds(qs, 256)], T1[s], put_other)

    class Reduce:
        def __init__(self, GP, RA, CB, RB, PB, RY, G, split):
            self.refs = GP, RA, CB, RB, PB, RY, G
            self.split = split
            self.live = {}

        def axes(self, h):
            return (x, xpeers, z, zpeers) if h == 0 else (z, zpeers, x, xpeers)

        def a_start(self, u, h):
            GP, RA = self.refs[:2]
            i, peers, _, _ = self.axes(h)
            self.live["a", u, h] = [
                send(
                    GP.at[u, :, pl.ds(pl.multiple_of(h * 512 + (i + k) % 4 * 128, 128), 128), :],
                    RA.at[u, h, k - 1], peers[k - 1],
                )
                for k in (1, 2, 3)
            ]

        def a_finish(self, u, h):
            GP, RA, CB = self.refs[:3]
            i, _, _, _ = self.axes(h)
            arrive(self.live["a", u, h])
            total = GP[u, :, pl.ds(pl.multiple_of(h * 512 + i * 128, 128), 128), :].astype(F32)
            for k in range(3):
                total = total + RA[u, h, k].astype(F32)
            CB[u, h] = total.astype(BF)

        def b_start(self, u, h):
            CB, RB = self.refs[2:4]
            _, _, j, peers = self.axes(h)
            self.live["b", u, h] = [
                send(
                    CB.at[u, h, :, pl.ds(pl.multiple_of((j + k) % 4 * 32, 32), 32), :],
                    RB.at[u, h, k - 1], peers[k - 1],
                )
                for k in (1, 2, 3)
            ]

        def b_finish(self, u, h, s):
            CB, RB, PB = self.refs[2:5]
            _, _, j, _ = self.axes(h)
            arrive(self.live["b", u, h])
            total = CB[u, h, :, pl.ds(pl.multiple_of(j * 32, 32), 32), :].astype(F32)
            for k in range(3):
                total = total + RB[u, h, k].astype(F32)
            PB[s, h] = total.astype(BF)

        def y_start(self, s, h):
            PB, RY = self.refs[4:6]
            self.live["y", s, h] = [
                send(PB.at[s, h], RY.at[s, h, k], ypeers[k]) for k in range(3)
            ]

        def place(self, s, h):
            G = self.refs[6]
            i, _, j, _ = self.axes(h)
            return G.at[s, :, pl.ds(pl.multiple_of(h * 512 + i * 128 + j * 32, 32), 32), :]

        def y_finish(self, s, h):
            PB, RY, G = self.refs[4:7]
            arrive(self.live["y", s, h])
            i, _, j, _ = self.axes(h)
            at = pl.ds(pl.multiple_of(h * 512 + i * 128 + j * 32, 32), 32)
            got = [RY[s, h, k].astype(F32) for k in range(3)]
            own = PB[s, h].astype(F32)
            if self.split:
                G[s, Y, at, :] = (own + got[1])[0].astype(BF)
                G[s, oY, at, :] = (got[0] + got[2])[0].astype(BF)
            else:
                G[s, :, at, :] = (own + got[0] + (got[1] + got[2])).astype(BF)

        def gb_start(self, s, h):
            _, _, _, peers = self.axes(h)
            at = self.place(s, h)
            self.live["gb", s, h] = [send(at, at, to) for to in peers]

        def gb_finish(self, s, h):
            arrive(self.live["gb", s, h])

        def ga_start(self, s, h):
            G = self.refs[6]
            i, peers, _, _ = self.axes(h)
            at = G.at[s, :, pl.ds(pl.multiple_of(h * 512 + i * 128, 128), 128), :]
            self.live["ga", s, h] = [send(at, at, to) for to in peers]

        def ga_finish(self, s, h):
            arrive(self.live["ga", s, h])

    first = Reduce(GP1, RA1, CB1, RB1, PB1, RY1, G1, True)
    second = Reduce(GP2, RA2, CB2, RB2, PB2, RY2, G2, False)

    def left(cc, yy, start, n):
        return WB[cc, yy, 0, pl.ds(start, n)].reshape(n * 128, 384)

    def right(cc, yy, s):
        return WB[cc, yy, 1, 2 * s + c].reshape(128, 384)

    def middle(it, get):
        MID[it, 0] = jnp.zeros((8, 1536), F32)

        def body(pb, _):
            cc, yy = pb % 2, pb // 2
            r0, r1 = right(cc, yy, 0), right(cc, yy, 1)
            lanes = pl.ds(pl.multiple_of(pb * 384, 128), 384)
            for i in range(2):
                total = jnp.zeros((1, 384), F32)
                for h in range(2):
                    proj = jnp.dot(get(0, i * 512 + h * 256), r0, preferred_element_type=F32)
                    proj = proj + jnp.dot(get(1, i * 512 + h * 256), r1, preferred_element_type=F32)
                    lf = left(cc, yy, 2 * h, 2).astype(F32)
                    total = total + jnp.sum(proj * lf, axis=0, keepdims=True)
                MID[it, 0, pl.ds(i, 1), lanes] = total
            return 0

        lax.fori_loop(0, 4, body, 0)
        return send(MID.at[it, 0], MID.at[it, 1], core)

    def ladder(it, copy):
        copy.wait_recv()

        for pb in range(4):
            cc, yy = pb % 2, pb // 2
            lanes = pl.ds(pb * 384, 384)

            def body(i, _):
                mid = MID[it, 0, pl.ds(i, 1), lanes] + MID[it, 1, pl.ds(i, 1), lanes]
                lf = left(cc, yy, 0, 4)
                at = pl.ds(pl.multiple_of(i * 512, 512), 512)
                for s in range(2):
                    wr = (right(cc, yy, s).astype(F32) * mid).astype(BF)
                    term = lax.dot_general(lf, wr, NT, preferred_element_type=F32)
                    if pb == 0:
                        LAD[s, at, :] = term
                    else:
                        LAD[s, at, :] = LAD[s, at, :] + term
                return 0

            lax.fori_loop(0, 2, body, 0)

    def update(G, s, put):
        def body(n, _):
            at = pl.multiple_of(n * 256, 256)
            here = pl.ds(at, 256)
            mine = pl.ds(pl.multiple_of(Y * 1024 + at, 256), 256)
            total = None
            for cc in range(2):
                q = pl.ds(cc * 512, 512)
                term = jnp.dot(BQ[cc, mine, :], G[s, Y, q, :], preferred_element_type=F32)
                total = term if total is None else total + term
            for cc in range(2):
                q = pl.ds(cc * 512, 512)
                total = total + jnp.dot(BR[cc, here, :], G[s, oY, q, :], preferred_element_type=F32)
            total = total + LAD[s, here, :]
            va = VA[pl.ds(pl.multiple_of(n % 2 * 256, 256), 256), :]
            vb = vir[0:1, pl.ds(pl.multiple_of((2 * s + c) * 128, 128), 128)]
            denom = va + vb - occ[2 * Y + n // 2] - piv[0]
            put(here, ((C[s, here, :].astype(F32) + total) / denom).astype(BF))
            return 0

        lax.fori_loop(0, 4, body, 0)

    halves = (0, 1)
    units = [(s, h) for s in range(2) for h in halves]

    for copy in lcopies:
        copy.wait()
    gram1(0, Y, c)
    for q in range(4):
        row = vir[0:1, q * 128:(q + 1) * 128]
        VA[q * 128:(q + 1) * 128, :] = jnp.transpose(jnp.broadcast_to(row, (128, 128)))
    arrive([b_in])
    gram1(0, Y, oc)
    for h in halves:
        first.a_start(0, h)
    arrive(thc_y)
    lx = [send(WB.at[c, :, 0, z, :, x], WB.at[c, :, 0, z, :, x], to) for to in xpeers]
    rz = [send(WB.at[c, :, 1, z, :, x], WB.at[c, :, 1, z, :, x], to) for to in zpeers]
    for h in halves:
        first.a_finish(0, h)
        first.b_start(0, h)
    arrive(lx)
    lz = [send(WB.at[c, :, 0, z], WB.at[c, :, 0, z], to) for to in zpeers]
    arrive(rz)
    rx = [send(WB.at[c, :, 1, :, :, x], WB.at[c, :, 1, :, :, x], to) for to in xpeers]
    for h in halves:
        first.b_finish(0, h, Y)
    arrive([t_in])
    gram1(1, oY, c)
    gram1(1, oY, oc)
    for h in halves:
        first.a_start(1, h)
    arrive(lz)
    arrive(rx)
    thc_core = [send(WB.at[c, :, 0], WB.at[c, :, 0], core)]
    for k in range(2):
        at = WB.at[c, :, 1, oc + 2 * k]
        thc_core.append(send(at, at, core))
    for h in halves:
        first.a_finish(1, h)
        first.b_start(1, h)
    arrive(thc_core)
    for h in halves:
        first.b_finish(1, h, oY)
    for s, h in units:
        first.y_start(s, h)
    moved += [move(n) for n in range(N_CHUNK // 2, N_CHUNK)]
    mid_copy = middle(0, lambda s, at: T0[s, pl.ds(pl.multiple_of(rows + at, 256), 256), :])
    for s, h in units:
        first.y_finish(s, h)
        first.gb_start(s, h)
    forwarded = []
    for n in range(N_CHUNK // 2):
        arrive([moved[n]])
        forwarded.append(forward(n))
    for s, h in units:
        first.gb_finish(s, h)
        first.ga_start(s, h)
    ladder(0, mid_copy)
    for n in range(N_CHUNK // 2, N_CHUNK):
        arrive([moved[n]])
        forwarded.append(forward(n))
    arrive(forwarded)

    for s in range(2):
        for h in halves:
            first.ga_finish(s, h)

        def put(here, value):
            T1[s, here, :] = value

        update(G1, s, put)
        gram2(s)
        for h in halves:
            second.a_start(s, h)

    mid_copy = middle(1, lambda s, at: T1[s, pl.ds(at, 256), :])
    for s, h in units:
        second.a_finish(s, h)
        second.b_start(s, h)
    for s, h in units:
        second.b_finish(s, h, s)
        second.y_start(s, h)
    ladder(1, mid_copy)
    for s, h in units:
        second.y_finish(s, h)
        second.gb_start(s, h)
    for s, h in units:
        second.gb_finish(s, h)
        second.ga_start(s, h)
    for s in range(2):
        for h in halves:
            second.ga_finish(s, h)

        def put(here, value):
            TS[s, here, :] = value

        update(G2, s, put)
    last = send(TS.at[oY], out.at[pl.ds(rows, 1024), :], ypeers[0])
    out[pl.ds(rows, 1024), :] = TS[Y]
    last.wait_recv()
    for copy in started:
        copy.wait_send()


def per_device(amplitudes, coulomb, df_factors, thc_left, thc_right, occ, vir, pivot):
    any_ = pl.BlockSpec(memory_space=pl.ANY)
    smem = pl.BlockSpec(memory_space=pltpu.SMEM)
    vmem = pl.BlockSpec(memory_space=pltpu.VMEM)

    def reduce_scratch(m):
        return [
            pltpu.VMEM((2, m, 1024, 128), BF),
            pltpu.VMEM((2, 2, 3, m, 128, 128), BF),
            pltpu.VMEM((2, 2, m, 128, 128), BF),
            pltpu.VMEM((2, 2, 3, m, 32, 128), BF),
            pltpu.VMEM((2, 2, m, 32, 128), BF),
            pltpu.VMEM((2, 2, 3, m, 32, 128), BF),
            pltpu.VMEM((2, 2, 1024, 128), BF),
        ]

    return pl.pallas_call(
        kernel,
        out_shape=jax.ShapeDtypeStruct((2048, 128), BF),
        in_specs=[any_] * 5 + [smem, vmem, smem],
        out_specs=vmem,
        scratch_shapes=[
            pltpu.VMEM((2, 2048, 512), BF),
            pltpu.VMEM((2, 1024, 512), BF),
            pltpu.VMEM((2, 2048, 128), BF),
            pltpu.VMEM((2, 1024, 128), BF),
            pltpu.VMEM((2, 1024, 128), BF),
            pltpu.VMEM((2, 1024, 128), BF),
            pltpu.VMEM((2, 1024, 128), F32),
            pltpu.VMEM((512, 128), F32),
            pltpu.VMEM((2, 2, 2, 4, 2, 4, 16, 384), BF),
            pltpu.VMEM((2, 2, 8, 1536), F32),
        ]
        + reduce_scratch(1)
        + reduce_scratch(2)
        + [
            pltpu.SemaphoreType.DMA((N_SEM,)),
            pltpu.SemaphoreType.DMA((N_SEM,)),
            pltpu.SemaphoreType.DMA((6,)),
        ],
        compiler_params=pltpu.CompilerParams(
            collective_id=0, has_side_effects=True, vmem_limit_bytes=56 * 2**20
        ),
    )(amplitudes, coulomb, df_factors, thc_left, thc_right, occ, vir.reshape(1, 512), pivot)


def solution(mesh):
    in_specs = (
        P("pair", "aux"),
        P("pair", None),
        P("pair", "aux"),
        P("pair", "aux"),
        P("pair", "aux"),
        P("pair"),
        P(),
        P(),
    )
    return jax.shard_map(
        per_device, mesh=mesh, in_specs=in_specs, out_specs=P("pair", "aux"), check_vma=False
    )
```

```python
import jax
import jax.numpy as jnp
from jax import lax
from jax.experimental import pallas as pl
from jax.experimental.pallas import tpu as pltpu
from jax.sharding import PartitionSpec as P

MESH = pl.DeviceIdType.MESH
BF = jnp.bfloat16
F32 = jnp.float32
N_SEM = 51
N_MOVE = 8
EARLY = 3
NT = (((1,), (1,)), ((), ()))


def mult(value, n):
    return pl.multiple_of(value, n)


def kernel(
    amps, coul, df, tl, tr, occ, vir, piv, out,
    BQ, BR, T0, TT0, TT1, TS, C, LAD, VA, WB, WR, MID,
    GF1, GP1, RA1, CB1, CF1, RB1, PB1, PF1, RY1, G1,
    GF2, GP2, RA2, CB2, CF2, RB2, PB2, PF2, RY2, G2,
    ss, rs, ls,
):
    a = lax.axis_index("aux")
    p = lax.axis_index("pair")
    Y, c = a // 2, a % 2
    z, yh, x = p // 8, (p // 4) % 2, p % 4
    oY, oc, oyh = 1 - Y, 1 - c, 1 - yh

    def dev(Y=Y, c=c, z=z, yh=yh, x=x):
        return {"aux": Y * 2 + c, "pair": z * 8 + yh * 4 + x}

    ypeers = [dev(Y=oY), dev(yh=oyh), dev(Y=oY, yh=oyh)]
    xpeers = [dev(x=(x + k) % 4) for k in (1, 2, 3)]
    zpeers = [dev(z=(z + k) % 4) for k in (1, 2, 3)]
    core = dev(c=oc)
    rows = mult(Y * 1024, 1024)
    orows = mult(oY * 1024, 1024)

    count = [0]
    groups = []

    class Group:
        def __init__(self, ruler):
            self.n, self.ruler = count[0], ruler
            count[0] += 1
            assert self.n < N_SEM
            groups.append(self)

        def send(self, src, dst, to):
            pltpu.make_async_remote_copy(
                src_ref=src, dst_ref=dst, send_sem=ss.at[self.n], recv_sem=rs.at[self.n],
                device_id=to, device_id_type=MESH,
            ).start()

        def arrive(self):
            pltpu.make_async_copy(self.ruler, self.ruler, rs.at[self.n]).wait()

        def sent(self):
            pltpu.make_async_copy(self.ruler, self.ruler, ss.at[self.n]).wait()

    def one(src, dst, to):
        group = Group(dst)
        group.send(src, dst, to)
        return group

    def to_all(src, dst, peers, ruler):
        group = Group(ruler)
        for to in peers:
            group.send(src, dst, to)
        return group

    piece = pl.ds(mult(c * 768 + Y * 384, 128), 384)
    plane = pl.ds(mult(c * 768, 128), 768)
    lcopies = []
    for n, (src, dst) in enumerate([
        (amps, T0.at[Y]),
        (df, BQ.at[c]),
        (tl, WB.at[0, z, yh, x, :, piece]),
        (tr, WB.at[1, z, yh, x, :, piece]),
        (coul.at[pl.ds(rows, 1024), pl.ds(mult(c * 128, 128), 128)], C.at[0]),
        (coul.at[pl.ds(rows, 1024), pl.ds(mult((2 + c) * 128, 128), 128)], C.at[1]),
    ]):
        copy = pltpu.make_async_copy(src, dst, ls.at[n])
        copy.start()
        lcopies.append(copy)

    barrier = pltpu.get_barrier_semaphore()
    for to in ypeers + xpeers + zpeers + [core]:
        pl.semaphore_signal(barrier, inc=1, device_id=to, device_id_type=MESH)

    def transpose0(s, half):
        for n in range(2):
            at = pl.ds(half * 1024 + n * 512, 512)
            TT0[s, :, at] = jnp.transpose(T0[s, at, :])

    def gram1(f, s, cc, half):
        at = pl.ds(half * 1024, 1024)
        got = jnp.dot(TT0[s, :, at], BQ[cc, at, :], preferred_element_type=F32)
        for q in range(4):
            value = got[:, q * 128:(q + 1) * 128]
            if half == 1:
                value = GF1[f, 0, cc * 4 + q] + value
                GP1[f, 0, cc * 4 + q] = value.astype(BF)
            GF1[f, 0, cc * 4 + q] = value

    lcopies[0].wait()
    transpose0(Y, 0)
    transpose0(Y, 1)
    for q in range(4):
        row = vir[0:1, q * 128:(q + 1) * 128]
        VA[q * 128:(q + 1) * 128, :] = jnp.transpose(jnp.broadcast_to(row, (128, 128)))
    lcopies[1].wait()
    gram1(0, Y, c, 0)
    gram1(0, Y, c, 1)
    pl.semaphore_wait(barrier, 10)

    b_in = one(df, BQ.at[c], core)
    thc_y = Group(WB.at[0, 0, 0, pl.ds(0, 2), :, pl.ds(0, 1152)])
    for to in ypeers:
        thc_y.send(tl, WB.at[0, z, yh, x, :, piece], to)
        thc_y.send(tr, WB.at[1, z, yh, x, :, piece], to)
    t_in = []
    for half in range(2):
        at = pl.ds(half * 1024, 1024)
        t_in.append(one(amps.at[at, :], T0.at[Y, at, :], ypeers[0]))
    size = 1024 // N_MOVE
    moved = []

    def move(count):
        for n in range(len(moved), len(moved) + count):
            src = df.at[pl.ds(mult(oY * 1024 + n * size, size), size), :]
            dst = BR.at[c, pl.ds(n * size, size), :]
            group = Group(BR.at[0, pl.ds(n * size, size), :])
            group.send(src, dst, ypeers[0])
            moved.append(group)

    forwarded = []

    def forward(count):
        start = len(forwarded) * 2
        for n in range(start, start + count * 2, 2):
            moved[n].arrive()
            moved[n + 1].arrive()
            block = BR.at[c, pl.ds(n * size, 2 * size), :]
            forwarded.append(one(block, block, core))

    class Reduce:
        def __init__(self, refs, split):
            self.GF, self.GP, self.RA, self.CB, self.CF = refs[:5]
            self.RB, self.PB, self.PF, self.RY, self.G = refs[5:]
            self.split = split
            self.live = {}

        def axes(self, h):
            return (x, xpeers, z, zpeers) if h == 0 else (z, zpeers, x, xpeers)

        def a_start(self, u, h):
            i, peers, _, _ = self.axes(h)
            group = self.live["a", u, h] = Group(self.RA.at[u, h])
            for k in (1, 2, 3):
                src = self.GP.at[u, :, h * 4 + (i + k) % 4]
                group.send(src, self.RA.at[u, h, k - 1], peers[k - 1])

        def a_finish(self, u):
            group = self.live["b", u] = Group(self.RB.at[u])
            for h in range(2):
                self.live["a", u, h].arrive()
                i, _, j, peers = self.axes(h)
                total = self.GF[u, :, h * 4 + i]
                for k in range(3):
                    total = total + self.RA[u, h, k].astype(F32)
                self.CF[u, h] = total
                self.CB[u, h] = total.astype(BF)
                for k in (1, 2, 3):
                    src = self.CB.at[u, h, :, pl.ds(mult((j + k) % 4 * 32, 32), 32), :]
                    group.send(src, self.RB.at[u, h, k - 1], peers[k - 1])

        def b_finish(self, u, s):
            self.live["b", u].arrive()
            for h in range(2):
                _, _, j, _ = self.axes(h)
                total = self.CF[u, h, :, pl.ds(mult(j * 32, 32), 32), :]
                for k in range(3):
                    total = total + self.RB[u, h, k].astype(F32)
                self.PF[s, h] = total
                self.PB[s, h] = total.astype(BF)

        def y_start(self, s):
            group = self.live["y", s] = Group(self.RY.at[s])
            for h in range(2):
                for k in range(3):
                    group.send(self.PB.at[s, h], self.RY.at[s, h, k], ypeers[k])

        def y_finish(self, s):
            self.live["y", s].arrive()
            group = self.live["gb", s] = Group(RB2.at[0])
            for h in range(2):
                i, _, j, peers = self.axes(h)
                at = pl.ds(mult(j * 32, 32), 32)
                got = [self.RY[s, h, k].astype(F32) for k in range(3)]
                own = self.PF[s, h]
                if self.split:
                    self.G[s, Y, h * 4 + i, at, :] = (own + got[1])[0].astype(BF)
                    self.G[s, oY, h * 4 + i, at, :] = (got[0] + got[2])[0].astype(BF)
                else:
                    self.G[s, :, h * 4 + i, at, :] = (own + got[0] + (got[1] + got[2])).astype(BF)
                place = self.G.at[s, :, h * 4 + i, at, :]
                for to in peers:
                    group.send(place, place, to)

        def gb_finish(self, s):
            self.live["gb", s].arrive()

        def ga_start(self, s, key):
            group = self.live["ga", key] = Group(RA2.at[0])
            for h in range(2):
                i, peers, _, _ = self.axes(h)
                place = self.G.at[s, :, h * 4 + i]
                for to in peers:
                    group.send(place, place, to)

        def ga_finish(self, key):
            self.live["ga", key].arrive()

    first = Reduce((GF1, GP1, RA1, CB1, CF1, RB1, PB1, PF1, RY1, G1), True)
    second = Reduce((GF2, GP2, RA2, CB2, CF2, RB2, PB2, PF2, RY2, G2), False)

    def left(start, n, lanes):
        return WB[0, pl.ds(start, n), :, :, :, lanes].reshape(n * 128, -1)

    def right(s, lanes):
        return WB[1, 2 * s + c, :, :, :, lanes].reshape(128, -1)

    def middle(it, get):
        MID[it, 0] = jnp.zeros((8, 1536), F32)

        def body(n, _):
            lanes = pl.ds(mult(n * 512, 512), 512)
            for i in range(2):
                inner = jnp.dot(get(i), left(0, 4, lanes), preferred_element_type=F32)
                total = jnp.sum(inner[:128] * right(0, lanes).astype(F32), axis=0, keepdims=True)
                total = total + jnp.sum(
                    inner[128:] * right(1, lanes).astype(F32), axis=0, keepdims=True
                )
                MID[it, 0, pl.ds(i, 1), lanes] = total
            return 0

        lax.fori_loop(0, 3, body, 0)
        return one(MID.at[it, 0], MID.at[it, 1], core)

    def ladder(it, group):
        group.arrive()
        for i in range(2):
            for n in range(3):
                lanes = pl.ds(n * 512, 512)
                mid = MID[it, 0, i:i + 1, lanes] + MID[it, 1, i:i + 1, lanes]
                for s in range(2):
                    wr = right(s, lanes).astype(F32) * mid
                    WR[i, s * 128:(s + 1) * 128, lanes] = wr.astype(BF)

        def body(n, _):
            lf = left(n % 2 * 2, 2, pl.ds(0, 1536))
            LAD[pl.ds(mult(n * 256, 256), 256), :] = lax.dot_general(
                lf, WR[n // 2], NT, preferred_element_type=F32
            )
            return 0

        lax.fori_loop(0, 4, body, 0)

    def cycle(G, n, stages):
        here = pl.ds(mult(n * 256, 256), 256)
        mine = pl.ds(mult(Y * 1024 + n * 256, 256), 256)
        total = None
        for src, at, yy in ((BQ, mine, Y), (BR, here, oY)):
            for cc in range(2):
                blocks = [
                    jnp.concatenate([G[s, yy, cc * 4 + q] for q in range(4)], axis=1)
                    for s in stages
                ]
                weight = blocks[0] if len(blocks) == 1 else jnp.concatenate(blocks, axis=0)
                term = lax.dot_general(src[cc, at, :], weight, NT, preferred_element_type=F32)
                total = term if total is None else total + term
        return here, total

    def finish(n, here, s, lad, total):
        va = VA[pl.ds(mult(n % 2 * 256, 256), 256), :]
        vb = vir[0:1, pl.ds(mult((2 * s + c) * 128, 128), 128)]
        denom = va + vb - occ[2 * Y + n // 2] - piv[0]
        return ((C[s, here, :].astype(F32) + (total + lad)) / denom).astype(BF)

    b_in.arrive()
    gram1(0, Y, oc, 0)
    gram1(0, Y, oc, 1)
    for h in range(2):
        first.a_start(0, h)
    for copy in lcopies[2:]:
        copy.wait()
    thc_y.arrive()
    wide = WB.at[0, 0, :, pl.ds(0, 3), :, pl.ds(0, 768)]
    lx = to_all(WB.at[0, z, :, x, :, plane], WB.at[0, z, :, x, :, plane], xpeers, wide)
    rz = to_all(WB.at[1, z, :, x, :, plane], WB.at[1, z, :, x, :, plane], zpeers, wide)
    first.a_finish(0)
    lx.arrive()
    rz.arrive()
    thc = []

    def spread(part):
        lanes = pl.ds(mult(c * 768 + part * 384, 128), 384)
        ruler = WB.at[0, pl.ds(0, 3), :, :, :, pl.ds(0, 384)]
        src = WB.at[0, z, :, :, :, lanes]
        thc.append(to_all(src, src, zpeers, ruler))
        src = WB.at[1, :, :, x, :, lanes]
        thc.append(to_all(src, src, xpeers, ruler))

    spread(0)
    first.b_finish(0, Y)
    move(EARLY)
    for half in range(2):
        t_in[half].arrive()
        transpose0(oY, half)
        gram1(1, oY, 0, half)
        if half == 1:
            first.a_start(1, 0)
        gram1(1, oY, 1, half)
    first.a_start(1, 1)
    first.a_finish(1)
    spread(1)
    first.b_finish(1, oY)
    for s in range(2):
        first.y_start(s)
    move(N_MOVE - EARLY)
    for group in thc:
        group.arrive()
    thc_core = [one(WB.at[0, :, :, :, :, plane], WB.at[0, :, :, :, :, plane], core)]
    group = Group(WB.at[1, pl.ds(0, 2), :, :, :, pl.ds(0, 768)])
    for k in range(2):
        place = WB.at[1, oc + 2 * k, :, :, :, plane]
        group.send(place, place, core)
    thc_core.append(group)
    for s in range(2):
        first.y_finish(s)
    for group in thc_core:
        group.arrive()
    mid = middle(0, lambda i: TT0[:, :, pl.ds(mult(rows + i * 512, 512), 512)].reshape(256, 512))
    for s in range(2):
        first.gb_finish(s)
        first.ga_start(s, s)
    ladder(0, mid)
    forward(N_MOVE // 2)
    for s in range(2):
        first.ga_finish(s)
    for group in forwarded:
        group.arrive()

    def update1(n, _):
        here, total = cycle(G1, n, (0, 1))
        for s in range(2):
            at = slice(s * 128, (s + 1) * 128)
            value = finish(n, here, s, LAD[here, at], total[:, at])
            TT1[s, :, here] = jnp.transpose(value)
        return 0

    lax.fori_loop(0, 4, update1, 0)

    for cc in range(2):
        for src, at, yy in ((BQ, pl.ds(rows, 1024), Y), (BR, pl.ds(0, 1024), oY)):
            got = jnp.dot(
                TT1[...].reshape(256, 1024), src[cc, at, :], preferred_element_type=F32
            )
            for s in range(2):
                for q in range(4):
                    value = got[s * 128:(s + 1) * 128, q * 128:(q + 1) * 128]
                    GF2[s, yy, cc * 4 + q] = value
                    GP2[s, yy, cc * 4 + q] = value.astype(BF)
        for s in range(2):
            second.a_start(s, cc)
    mid = middle(1, lambda i: TT1[:, :, pl.ds(i * 512, 512)].reshape(256, 512))
    ladder(1, mid)
    for s in range(2):
        second.a_finish(s)
    for s in range(2):
        second.b_finish(s, s)
        second.y_start(s)
    for s in range(2):
        second.y_finish(s)
    for s in range(2):
        second.gb_finish(s)
    second.ga_start(oY, 0)
    second.ga_start(Y, 1)

    second.ga_finish(0)
    last = Group(TS)
    for n in range(4):
        here, total = cycle(G2, n, (oY,))
        lad = LAD[here, pl.ds(mult(oY * 128, 128), 128)]
        TS[here, :] = finish(n, here, oY, lad, total)
        last.send(TS.at[here, :], out.at[pl.ds(mult(Y * 1024 + n * 256, 256), 256), :], ypeers[0])
    second.ga_finish(1)

    def update2(n, _):
        here, total = cycle(G2, n, (Y,))
        lad = LAD[here, pl.ds(mult(Y * 128, 128), 128)]
        out[pl.ds(mult(Y * 1024 + n * 256, 256), 256), :] = finish(n, here, Y, lad, total)
        return 0

    lax.fori_loop(0, 4, update2, 0)
    last.arrive()
    for group in groups:
        group.sent()


def per_device(amplitudes, coulomb, df_factors, thc_left, thc_right, occ, vir, pivot):
    any_ = pl.BlockSpec(memory_space=pl.ANY)
    smem = pl.BlockSpec(memory_space=pltpu.SMEM)
    vmem = pl.BlockSpec(memory_space=pltpu.VMEM)

    def reduce_scratch(m):
        return [
            pltpu.VMEM((2, m, 8, 128, 128), F32),
            pltpu.VMEM((2, m, 8, 128, 128), BF),
            pltpu.VMEM((2, 2, 3, m, 128, 128), BF),
            pltpu.VMEM((2, 2, m, 128, 128), BF),
            pltpu.VMEM((2, 2, m, 128, 128), F32),
            pltpu.VMEM((2, 2, 3, m, 32, 128), BF),
            pltpu.VMEM((2, 2, m, 32, 128), BF),
            pltpu.VMEM((2, 2, m, 32, 128), F32),
            pltpu.VMEM((2, 2, 3, m, 32, 128), BF),
            pltpu.VMEM((2, 2, 8, 128, 128), BF),
        ]

    return pl.pallas_call(
        kernel,
        out_shape=jax.ShapeDtypeStruct((2048, 128), BF),
        in_specs=[any_] * 5 + [smem, vmem, smem],
        out_specs=vmem,
        scratch_shapes=[
            pltpu.VMEM((2, 2048, 512), BF),
            pltpu.VMEM((2, 1024, 512), BF),
            pltpu.VMEM((2, 2048, 128), BF),
            pltpu.VMEM((2, 128, 2048), BF),
            pltpu.VMEM((2, 128, 1024), BF),
            pltpu.VMEM((1024, 128), BF),
            pltpu.VMEM((2, 1024, 128), BF),
            pltpu.VMEM((1024, 256), F32),
            pltpu.VMEM((512, 128), F32),
            pltpu.VMEM((2, 4, 2, 4, 16, 1536), BF),
            pltpu.VMEM((2, 256, 1536), BF),
            pltpu.VMEM((2, 2, 8, 1536), F32),
        ]
        + reduce_scratch(1)
        + reduce_scratch(2)
        + [
            pltpu.SemaphoreType.DMA((N_SEM,)),
            pltpu.SemaphoreType.DMA((N_SEM,)),
            pltpu.SemaphoreType.DMA((6,)),
        ],
        compiler_params=pltpu.CompilerParams(
            collective_id=0, has_side_effects=True, vmem_limit_bytes=56 * 2**20
        ),
    )(amplitudes, coulomb, df_factors, thc_left, thc_right, occ, vir.reshape(1, 512), pivot)


def solution(mesh):
    in_specs = (
        P("pair", "aux"),
        P("pair", None),
        P("pair", "aux"),
        P("pair", "aux"),
        P("pair", "aux"),
        P("pair"),
        P(),
        P(),
    )
    return jax.shard_map(
        per_device, mesh=mesh, in_specs=in_specs, out_specs=P("pair", "aux"), check_vma=False
    )
```

```python
import jax
import jax.numpy as jnp
from jax import lax
from jax.experimental import pallas as pl
from jax.experimental.pallas import tpu as pltpu
from jax.sharding import PartitionSpec as P

MESH = pl.DeviceIdType.MESH
BF = jnp.bfloat16
F32 = jnp.float32
N_SEM = 57
N_MOVE = 8
EARLY = 4
NT = (((1,), (1,)), ((), ()))


def mult(value, n):
    return pl.multiple_of(value, n)


def kernel(
    amps, coul, df, tl, tr, occ, vir, piv, out,
    BQ, BR, T0, TT0, TT1, T1, TS, C, LAD, VA, WB, WR, MID,
    GF1, GP1, RA1, CB1, CF1, RB1, PB1, PF1, RY1, G1,
    GF2, GP2, RA2, CB2, CF2, RB2, PB2, PF2, RY2, G2,
    ss, rs, ls,
):
    a = lax.axis_index("aux")
    p = lax.axis_index("pair")
    Y, c = a // 2, a % 2
    z, yh, x = p // 8, (p // 4) % 2, p % 4
    oY, oc, oyh = 1 - Y, 1 - c, 1 - yh

    def dev(Y=Y, c=c, z=z, yh=yh, x=x):
        return {"aux": Y * 2 + c, "pair": z * 8 + yh * 4 + x}

    ypeers = [dev(Y=oY), dev(yh=oyh), dev(Y=oY, yh=oyh)]
    yring = [dev(Y=(yh * 2 + Y + k) % 2, yh=(yh * 2 + Y + k) % 4 // 2) for k in (1, 2, 3)]
    xpeers = [dev(x=(x + k) % 4) for k in (1, 2, 3)]
    zpeers = [dev(z=(z + k) % 4) for k in (1, 2, 3)]
    core = dev(c=oc)
    blocks = [c, 1 - c]
    rows = mult(Y * 1024, 1024)
    orows = mult(oY * 1024, 1024)

    count = [0]
    groups = []

    class Group:
        def __init__(self, ruler):
            self.n, self.ruler = count[0], ruler
            count[0] += 1
            assert self.n < N_SEM
            groups.append(self)

        def send(self, src, dst, to):
            pltpu.make_async_remote_copy(
                src_ref=src, dst_ref=dst, send_sem=ss.at[self.n], recv_sem=rs.at[self.n],
                device_id=to, device_id_type=MESH,
            ).start()

        def arrive(self):
            pltpu.make_async_copy(self.ruler, self.ruler, rs.at[self.n]).wait()

        def sent(self):
            pltpu.make_async_copy(self.ruler, self.ruler, ss.at[self.n]).wait()

    def one(src, dst, to):
        group = Group(dst)
        group.send(src, dst, to)
        return group

    def to_all(src, dst, peers, ruler):
        group = Group(ruler)
        for to in peers:
            group.send(src, dst, to)
        return group

    piece = pl.ds(mult(c * 768 + Y * 384, 128), 384)
    plane = pl.ds(mult(c * 768, 128), 768)
    lcopies = []
    for n, (src, dst) in enumerate([
        (amps, T0.at[Y]),
        (df, BQ.at[c]),
        (tl, WB.at[0, z, yh, x, :, piece]),
        (tr, WB.at[1, z, yh, x, :, piece]),
        (coul.at[pl.ds(rows, 1024), pl.ds(mult((2 * blocks[0] + c) * 128, 128), 128)], C.at[0]),
        (coul.at[pl.ds(rows, 1024), pl.ds(mult((2 * blocks[1] + c) * 128, 128), 128)], C.at[1]),
    ]):
        copy = pltpu.make_async_copy(src, dst, ls.at[n])
        copy.start()
        lcopies.append(copy)

    barrier = pltpu.get_barrier_semaphore()
    for to in ypeers + xpeers + zpeers + [core]:
        pl.semaphore_signal(barrier, inc=1, device_id=to, device_id_type=MESH)

    def transpose0(s, half):
        for n in range(2):
            at = pl.ds(half * 1024 + n * 512, 512)
            TT0[s, :, at] = jnp.transpose(T0[s, at, :])

    def gram1(f, s, cc, half):
        at = pl.ds(half * 1024, 1024)
        got = jnp.dot(TT0[s, :, at], BQ[cc, at, :], preferred_element_type=F32)
        for q in range(4):
            value = got[:, q * 128:(q + 1) * 128]
            if half == 1:
                value = GF1[f, 0, cc * 4 + q] + value
                GP1[f, 0, cc * 4 + q] = value.astype(BF)
            GF1[f, 0, cc * 4 + q] = value

    pl.semaphore_wait(barrier, 10)

    b_in = one(df, BQ.at[c], core)
    thc_y = Group(WB.at[0, 0, 0, pl.ds(0, 2), :, pl.ds(0, 1152)])
    for to in ypeers:
        thc_y.send(tl, WB.at[0, z, yh, x, :, piece], to)
        thc_y.send(tr, WB.at[1, z, yh, x, :, piece], to)
    t_in = []
    for half in range(2):
        at = pl.ds(half * 1024, 1024)
        t_in.append(one(amps.at[at, :], T0.at[Y, at, :], ypeers[0]))

    lcopies[0].wait()
    transpose0(Y, 0)
    transpose0(Y, 1)
    for q in range(4):
        row = vir[0:1, q * 128:(q + 1) * 128]
        VA[q * 128:(q + 1) * 128, :] = jnp.transpose(jnp.broadcast_to(row, (128, 128)))
    lcopies[1].wait()
    gram1(0, Y, c, 0)
    gram1(0, Y, c, 1)

    size = 1024 // N_MOVE
    moved = [Group(BR.at[0, pl.ds(n * size, size), :]) for n in range(N_MOVE)]

    def move(start, stop):
        for n in range(start, stop):
            src = df.at[pl.ds(mult(oY * 1024 + n * size, size), size), :]
            moved[n].send(src, BR.at[c, pl.ds(n * size, size), :], ypeers[0])

    forwarded = []

    def forward(count):
        start = len(forwarded) * 2
        for n in range(start, start + count * 2, 2):
            moved[n].arrive()
            moved[n + 1].arrive()
            block = BR.at[c, pl.ds(n * size, 2 * size), :]
            forwarded.append(one(block, block, core))

    class Reduce:
        def __init__(self, refs, split, gb_ruler, ga_ruler):
            self.GF, self.GP, self.RA, self.CB, self.CF = refs[:5]
            self.RB, self.PB, self.PF, self.RY, self.G = refs[5:]
            self.split, self.gb_ruler, self.ga_ruler = split, gb_ruler, ga_ruler
            self.part = self.GP.shape[3] // 4
            self.live = {}

        def axes(self, u, h):
            if u == 3:
                return (yh * 2 + Y, yring) + ((x, xpeers, zpeers) if h == 0 else (z, zpeers, xpeers))
            return ((x, xpeers, z, zpeers) if h == 0 else (z, zpeers, x, xpeers)) + (ypeers,)

        def own(self, j):
            return pl.ds(mult(j * self.part, self.part), self.part)

        def a_start(self, u, h):
            i, peers, _, _, _ = self.axes(u, h)
            if ("a", u) not in self.live:
                self.live["a", u] = Group(self.RA.at[u])
            for k in (1, 2, 3):
                src = self.GP.at[u, :, h * 4 + (i + k) % 4]
                self.live["a", u].send(src, self.RA.at[u, h, k - 1], peers[k - 1])

        def a_finish(self, u):
            self.live["a", u].arrive()
            group = self.live["b", u] = Group(self.RB.at[u])
            for h in range(2):
                i, _, j, peers, _ = self.axes(u, h)
                total = self.GF[u, :, h * 4 + i]
                for k in range(3):
                    total = total + self.RA[u, h, k].astype(F32)
                self.CF[u, h] = total
                self.CB[u, h] = total.astype(BF)
                for k in (1, 2, 3):
                    src = self.CB.at[u, h, :, self.own((j + k) % 4), :]
                    group.send(src, self.RB.at[u, h, k - 1], peers[k - 1])

        def b_finish(self, u, s):
            self.live["b", u].arrive()
            for h in range(2):
                _, _, j, _, _ = self.axes(u, h)
                total = self.CF[u, h, :, self.own(j), :]
                for k in range(3):
                    total = total + self.RB[u, h, k].astype(F32)
                self.PF[s, h] = total
                self.PB[s, h] = total.astype(BF)

        def y_start(self, s):
            group = self.live["y", s] = Group(self.RY.at[s])
            for h in range(2):
                peers = ypeers if self.split else self.axes(s, h)[4]
                for k in range(3):
                    group.send(self.PB.at[s, h], self.RY.at[s, h, k], peers[k])

        def y_finish(self, s):
            self.live["y", s].arrive()
            group = self.live["gb", s] = Group(self.gb_ruler)
            for h in range(2):
                i, _, j, peers, _ = self.axes(s, h)
                at = self.own(j)
                got = [self.RY[s, h, k].astype(F32) for k in range(3)]
                own = self.PF[s, h]
                if self.split:
                    self.G[s, Y, h * 4 + i, at, :] = (own + got[1])[0].astype(BF)
                    self.G[s, oY, h * 4 + i, at, :] = (got[0] + got[2])[0].astype(BF)
                else:
                    self.G[s, :, h * 4 + i, at, :] = (own + got[0] + (got[1] + got[2])).astype(BF)
                place = self.G.at[s, :, h * 4 + i, at, :]
                for to in peers:
                    group.send(place, place, to)

        def gb_finish(self, s):
            self.live["gb", s].arrive()
            group = self.live["ga", s] = Group(self.ga_ruler)
            for h in range(2):
                i, peers, _, _, _ = self.axes(s, h)
                place = self.G.at[s, :, h * 4 + i]
                for to in peers:
                    group.send(place, place, to)

        def ga_finish(self, s):
            self.live["ga", s].arrive()

    first = Reduce(
        (GF1, GP1, RA1, CB1, CF1, RB1, PB1, PF1, RY1, G1), True, RA1.at[0, 0], RA1
    )
    second = Reduce(
        (GF2, GP2, RA2, CB2, CF2, RB2, PB2, PF2, RY2, G2), False, RB2.at[0], RA2.at[0]
    )

    def left(start, n, lanes):
        return WB[0, pl.ds(start, n), :, :, :, lanes].reshape(n * 128, -1)

    def right(s, lanes):
        return WB[1, 2 * s + c, :, :, :, lanes].reshape(128, -1)

    def middle(it, i, order, inner_of):
        def body(n, _):
            lanes = pl.ds(mult(n * 512, 512), 512)
            inner = jnp.dot(inner_of, left(0, 4, lanes), preferred_element_type=F32)
            total = jnp.sum(inner[:128] * right(order[0], lanes).astype(F32), axis=0, keepdims=True)
            total = total + jnp.sum(
                inner[128:] * right(order[1], lanes).astype(F32), axis=0, keepdims=True
            )
            MID[it, 0, i:i + 1, lanes] = total
            return 0

        lax.fori_loop(0, 3, body, 0)

    def share(it):
        return one(MID.at[it, 0], MID.at[it, 1], core)

    def ladder_weights(it, group):
        group.arrive()
        for i in range(2):
            for n in range(3):
                lanes = pl.ds(n * 512, 512)
                mid = MID[it, 0, i:i + 1, lanes] + MID[it, 1, i:i + 1, lanes]
                for k in range(2):
                    wr = right(blocks[k], lanes).astype(F32) * mid
                    WR[i, k * 128:(k + 1) * 128, lanes] = wr.astype(BF)

    def ladder(start, stop):
        def body(n, _):
            lf = left(n % 2 * 2, 2, pl.ds(0, 1536))
            LAD[pl.ds(mult(n * 256, 256), 256), :] = lax.dot_general(
                lf, WR[n // 2], NT, preferred_element_type=F32
            )
            return 0

        lax.fori_loop(start, stop, body, 0)

    def cycle(G, n, stages):
        here = pl.ds(mult(n * 256, 256), 256)
        mine = pl.ds(mult(Y * 1024 + n * 256, 256), 256)
        total = None
        for src, at, yy in ((BQ, mine, Y), (BR, here, oY)):
            for cc in range(2):
                weight = jnp.concatenate(
                    [
                        jnp.concatenate([G[s, yy, cc * 4 + q] for q in range(4)], axis=1)
                        for s in stages
                    ],
                    axis=0,
                )
                term = lax.dot_general(src[cc, at, :], weight, NT, preferred_element_type=F32)
                total = term if total is None else total + term
        return here, total

    def finish(n, here, k, total):
        va = VA[pl.ds(mult(n % 2 * 256, 256), 256), :]
        vb = vir[0:1, pl.ds(mult((2 * blocks[k] + c) * 128, 128), 128)]
        denom = va + vb - occ[2 * Y + n // 2] - piv[0]
        lad = LAD[here, k * 128:(k + 1) * 128]
        return ((C[k, here, :].astype(F32) + (total + lad)) / denom).astype(BF)

    b_in.arrive()
    gram1(0, Y, oc, 0)
    gram1(0, Y, oc, 1)
    for copy in lcopies[2:]:
        copy.wait()
    thc_y.arrive()
    wide = WB.at[0, 0, :, pl.ds(0, 3), :, pl.ds(0, 768)]
    lx = to_all(WB.at[0, z, :, x, :, plane], WB.at[0, z, :, x, :, plane], xpeers, wide)
    rz = to_all(WB.at[1, z, :, x, :, plane], WB.at[1, z, :, x, :, plane], zpeers, wide)
    for h in range(2):
        first.a_start(0, h)
    lx.arrive()
    rz.arrive()
    third = WB.at[0, pl.ds(0, 3), :, :, :, pl.ds(0, 384)]

    def spread(part, pair):
        lanes = pl.ds(mult(c * 768 + part * 384, 128), 384)
        for to in range(3):
            src = WB.at[0, z, :, :, :, lanes]
            pair[0].send(src, src, zpeers[to])
            src = WB.at[1, :, :, x, :, lanes]
            pair[1].send(src, src, xpeers[to])

    soon = [Group(third), Group(third)]
    spread(0, soon)
    first.a_finish(0)
    for half in range(2):
        t_in[half].arrive()
        transpose0(oY, half)
        gram1(1, oY, 0, half)
        if half == 0:
            move(0, EARLY)
        else:
            first.a_start(1, 0)
        gram1(1, oY, 1, half)
    first.a_start(1, 1)
    late = [Group(third), Group(third)]
    spread(1, late)
    first.b_finish(0, (Y + c) % 2)
    first.a_finish(1)
    first.b_finish(1, (oY + c) % 2)
    for k in range(2):
        first.y_start(k)

    @pl.when(c == 0)
    def _():
        move(EARLY, N_MOVE)

    for group in soon + late:
        group.arrive()
    thc_core = [one(WB.at[0, :, :, :, :, plane], WB.at[0, :, :, :, :, plane], core)]
    group = Group(WB.at[1, pl.ds(0, 2), :, :, :, pl.ds(0, 768)])
    for k in range(2):
        place = WB.at[1, oc + 2 * k, :, :, :, plane]
        group.send(place, place, core)
    thc_core.append(group)
    for k in range(2):
        first.y_finish(k)
    for k in range(2):
        first.gb_finish(k)

    @pl.when(c == 1)
    def _():
        move(EARLY, N_MOVE)

    for group in thc_core:
        group.arrive()
    MID[0, 0] = jnp.zeros((8, 1536), F32)
    MID[1, 0] = jnp.zeros((8, 1536), F32)
    for i in range(2):
        at = pl.ds(mult(rows + i * 512, 512), 512)
        middle(0, i, (0, 1), TT0[:, :, at].reshape(256, 512))
    mid = share(0)
    forward(2)
    ladder_weights(0, mid)
    ladder(0, 4)
    forward(2)
    for k in range(2):
        first.ga_finish(k)

    def update1(n):
        here, total = cycle(G1, n, (0, 1))
        for k in range(2):
            value = finish(n, here, k, total[:, k * 128:(k + 1) * 128])
            TT1[k, :, here] = jnp.transpose(value)

    def first_rows(n, _):
        update1(n)
        return 0

    for group in forwarded:
        group.arrive()
    lax.fori_loop(0, 4, first_rows, 0)

    def gram2(cc):
        for src, at, yy in ((BQ, pl.ds(rows, 1024), Y), (BR, pl.ds(0, 1024), oY)):
            got = jnp.dot(
                TT1[...].reshape(256, 1024), src[cc, at, :], preferred_element_type=F32
            )
            for j in range(4):
                for q in range(4):
                    value = got[j * 64:(j + 1) * 64, q * 128:(q + 1) * 128]
                    GF2[j, yy, cc * 4 + q] = value
                    GP2[j, yy, cc * 4 + q] = value.astype(BF)
        for j in range(4):
            second.a_start(j, cc)

    gram2(0)
    gram2(1)

    for i in range(2):
        middle(1, i, blocks, TT1[:, :, i * 512:(i + 1) * 512].reshape(256, 512))
    mid = share(1)
    steps = [
        ("a", 0), ("a", 1), ("l", 0), ("a", 2), ("a", 3), ("l", 1), ("b", 0), ("b", 1), ("l", 2),
        ("b", 2), ("l", 3), ("b", 3), ("y", 0), ("y", 1), ("l", 4), ("y", 2), ("y", 3),
        ("g", 0), ("g", 1), ("g", 2), ("g", 3),
    ]
    for step, j in steps:
        if step == "l":
            if j == 0:
                ladder_weights(1, mid)
            else:
                ladder(j - 1, j)
        elif step == "a":
            second.a_finish(j)
        elif step == "b":
            second.b_finish(j, j)
            second.y_start(j)
        elif step == "y":
            second.y_finish(j)
        else:
            second.gb_finish(j)

    last = Group(TS)
    for k in range(2):
        second.ga_finish(2 * k)
        second.ga_finish(2 * k + 1)
        for n in range(4):
            here, total = cycle(G2, n, (2 * k, 2 * k + 1))
            value = finish(n, here, k, total)
            there = out.at[pl.ds(mult(Y * 1024 + n * 256, 256), 256), :]

            @pl.when(blocks[k] == oY)
            def _():
                TS[here, :] = value
                last.send(TS.at[here, :], there, ypeers[0])

            @pl.when(blocks[k] == Y)
            def _():
                T1[here, :] = value
                pltpu.make_async_copy(T1.at[here, :], there, ls.at[6]).start()

    pltpu.make_async_copy(T1, out.at[pl.ds(rows, 1024), :], ls.at[6]).wait()
    last.arrive()
    for group in groups:
        group.sent()


def per_device(amplitudes, coulomb, df_factors, thc_left, thc_right, occ, vir, pivot):
    any_ = pl.BlockSpec(memory_space=pl.ANY)
    smem = pl.BlockSpec(memory_space=pltpu.SMEM)
    vmem = pl.BlockSpec(memory_space=pltpu.VMEM)

    def reduce_scratch(n, m, b):
        return [
            pltpu.VMEM((n, m, 8, b, 128), F32),
            pltpu.VMEM((n, m, 8, b, 128), BF),
            pltpu.VMEM((n, 2, 3, m, b, 128), BF),
            pltpu.VMEM((n, 2, m, b, 128), BF),
            pltpu.VMEM((n, 2, m, b, 128), F32),
            pltpu.VMEM((n, 2, 3, m, b // 4, 128), BF),
            pltpu.VMEM((n, 2, m, b // 4, 128), BF),
            pltpu.VMEM((n, 2, m, b // 4, 128), F32),
            pltpu.VMEM((n, 2, 3, m, b // 4, 128), BF),
            pltpu.VMEM((n, 2, 8, b, 128), BF),
        ]

    return pl.pallas_call(
        kernel,
        out_shape=jax.ShapeDtypeStruct((2048, 128), BF),
        in_specs=[any_] * 5 + [smem, vmem, smem],
        out_specs=any_,
        scratch_shapes=[
            pltpu.VMEM((2, 2048, 512), BF),
            pltpu.VMEM((2, 1024, 512), BF),
            pltpu.VMEM((2, 2048, 128), BF),
            pltpu.VMEM((2, 128, 2048), BF),
            pltpu.VMEM((2, 128, 1024), BF),
            pltpu.VMEM((1024, 128), BF),
            pltpu.VMEM((1024, 128), BF),
            pltpu.VMEM((2, 1024, 128), BF),
            pltpu.VMEM((1024, 256), F32),
            pltpu.VMEM((512, 128), F32),
            pltpu.VMEM((2, 4, 2, 4, 16, 1536), BF),
            pltpu.VMEM((2, 256, 1536), BF),
            pltpu.VMEM((2, 2, 8, 1536), F32),
        ]
        + reduce_scratch(2, 1, 128)
        + reduce_scratch(4, 2, 64)
        + [
            pltpu.SemaphoreType.DMA((N_SEM,)),
            pltpu.SemaphoreType.DMA((N_SEM,)),
            pltpu.SemaphoreType.DMA((7,)),
        ],
        compiler_params=pltpu.CompilerParams(
            collective_id=0, has_side_effects=True, vmem_limit_bytes=56 * 2**20
        ),
    )(amplitudes, coulomb, df_factors, thc_left, thc_right, occ, vir.reshape(1, 512), pivot)


def solution(mesh):
    in_specs = (
        P("pair", "aux"),
        P("pair", None),
        P("pair", "aux"),
        P("pair", "aux"),
        P("pair", "aux"),
        P("pair"),
        P(),
        P(),
    )
    return jax.shard_map(
        per_device, mesh=mesh, in_specs=in_specs, out_specs=P("pair", "aux"), check_vma=False
    )
```

```python
import jax
import jax.numpy as jnp
from jax import lax
from jax.experimental import pallas as pl
from jax.experimental.pallas import tpu as pltpu
from jax.sharding import PartitionSpec as P

MESH = pl.DeviceIdType.MESH
BF = jnp.bfloat16
F32 = jnp.float32
N_SEM = 57
N_SENT = 20
N_MOVE = 8
EARLY = 4
NT = (((1,), (1,)), ((), ()))


def mult(value, n):
    return pl.multiple_of(value, n)


def kernel(
    amps, coul, df, tl, tr, occ_in, vir_in, piv_in, out,
    BQ, BR, T0, TT0, TT1, T1, TS, C, LAD, VA, WB, WR, MID,
    GF1, GP1, RA1, CB1, CF1, RB1, PB1, PF1, RY1, G1,
    GF2, GP2, RA2, CB2, CF2, RB2, PB2, PF2, RY2, G2,
    ss, rs, ls, occ, vir, piv,
):
    a = lax.axis_index("aux")
    p = lax.axis_index("pair")
    Y, c = a // 2, a % 2
    z, yh, x = p // 8, (p // 4) % 2, p % 4
    oY, oc, oyh = 1 - Y, 1 - c, 1 - yh

    def dev(Y=Y, c=c, z=z, yh=yh, x=x):
        return {"aux": Y * 2 + c, "pair": z * 8 + yh * 4 + x}

    ypeers = [dev(Y=oY), dev(yh=oyh), dev(Y=oY, yh=oyh)]
    yring = [dev(Y=(yh * 2 + Y + k) % 2, yh=(yh * 2 + Y + k) % 4 // 2) for k in (1, 2, 3)]
    xpeers = [dev(x=(x + k) % 4) for k in (1, 2, 3)]
    zpeers = [dev(z=(z + k) % 4) for k in (1, 2, 3)]
    core = dev(c=oc)
    blocks = [c, 1 - c]
    rows = mult(Y * 1024, 1024)
    orows = mult(oY * 1024, 1024)

    count = [0]
    kinds = {}

    class Group:
        def __init__(self, ruler, kind=None, total=None):
            self.n, self.ruler = count[0], ruler
            count[0] += 1
            if kind not in kinds:
                kind = kind or str(self.n)
                kinds[kind] = len(kinds), ruler if total is None else total
            self.m = kinds[kind][0]
            assert self.n < N_SEM and self.m < N_SENT

        def send(self, src, dst, to):
            pltpu.make_async_remote_copy(
                src_ref=src, dst_ref=dst, send_sem=ss.at[self.m], recv_sem=rs.at[self.n],
                device_id=to, device_id_type=MESH,
            ).start()

        def arrive(self):
            pltpu.make_async_copy(self.ruler, self.ruler, rs.at[self.n]).wait()

    def one(src, dst, to, *kind):
        group = Group(dst, *kind)
        group.send(src, dst, to)
        return group

    def to_all(src, dst, peers, ruler, *kind):
        group = Group(ruler, *kind)
        for to in peers:
            group.send(src, dst, to)
        return group

    piece = pl.ds(mult(c * 768 + Y * 384, 128), 384)
    plane = pl.ds(mult(c * 768, 128), 768)
    lcopies = []
    for n, (src, dst) in enumerate([
        (amps, T0.at[Y]),
        (df, BQ.at[c]),
        (tl, WB.at[0, z, yh, x, :, piece]),
        (tr, WB.at[1, z, yh, x, :, piece]),
        (coul.at[pl.ds(rows, 1024), pl.ds(mult((2 * blocks[0] + c) * 128, 128), 128)], C.at[0]),
        (coul.at[pl.ds(rows, 1024), pl.ds(mult((2 * blocks[1] + c) * 128, 128), 128)], C.at[1]),
        (vir_in, vir),
        (occ_in, occ),
        (piv_in, piv),
    ]):
        copy = pltpu.make_async_copy(src, dst, ls.at[n])
        copy.start()
        lcopies.append(copy)

    barrier = pltpu.get_barrier_semaphore()
    for to in ypeers + xpeers + zpeers + [core]:
        pl.semaphore_signal(barrier, inc=1, device_id=to, device_id_type=MESH)

    def transpose0(s, half):
        for n in range(2):
            at = pl.ds(half * 1024 + n * 512, 512)
            TT0[s, :, at] = jnp.transpose(T0[s, at, :])

    def gram1(f, s, cc, half):
        at = pl.ds(half * 1024, 1024)
        got = jnp.dot(TT0[s, :, at], BQ[cc, at, :], preferred_element_type=F32)
        for q in range(4):
            value = got[:, q * 128:(q + 1) * 128]
            if half == 1:
                value = GF1[f, 0, cc * 4 + q] + value
                GP1[f, 0, cc * 4 + q] = value.astype(BF)
            GF1[f, 0, cc * 4 + q] = value

    pl.semaphore_wait(barrier, 10)

    b_in = one(df, BQ.at[c], core)
    thc_y = Group(WB.at[0, 0, 0, pl.ds(0, 2), :, pl.ds(0, 1152)])
    for to in ypeers:
        thc_y.send(tl, WB.at[0, z, yh, x, :, piece], to)
        thc_y.send(tr, WB.at[1, z, yh, x, :, piece], to)
    t_in = []
    for half in range(2):
        at = pl.ds(half * 1024, 1024)
        t_in.append(one(amps.at[at, :], T0.at[Y, at, :], ypeers[0], "t", T0.at[0]))

    lcopies[0].wait()
    transpose0(Y, 0)
    transpose0(Y, 1)
    lcopies[6].wait()
    for q in range(4):
        row = vir[0:1, q * 128:(q + 1) * 128]
        VA[q * 128:(q + 1) * 128, :] = jnp.transpose(jnp.broadcast_to(row, (128, 128)))
    lcopies[1].wait()
    gram1(0, Y, c, 0)
    gram1(0, Y, c, 1)

    size = 1024 // N_MOVE
    moved = [Group(BR.at[0, pl.ds(n * size, size), :], "move", BR.at[0]) for n in range(N_MOVE)]

    def move(start, stop):
        for n in range(start, stop):
            src = df.at[pl.ds(mult(oY * 1024 + n * size, size), size), :]
            moved[n].send(src, BR.at[c, pl.ds(n * size, size), :], ypeers[0])

    forwarded = []

    def forward(count):
        start = len(forwarded) * 2
        for n in range(start, start + count * 2, 2):
            moved[n].arrive()
            moved[n + 1].arrive()
            block = BR.at[c, pl.ds(n * size, 2 * size), :]
            forwarded.append(one(block, block, core, "forward", BR.at[0]))

    class Reduce:
        def __init__(self, name, refs, split, gb_ruler, gb_total, ga_ruler):
            self.name, self.gb_total = name, gb_total
            self.GF, self.GP, self.RA, self.CB, self.CF = refs[:5]
            self.RB, self.PB, self.PF, self.RY, self.G = refs[5:]
            self.split, self.gb_ruler, self.ga_ruler = split, gb_ruler, ga_ruler
            self.part = self.GP.shape[3] // 4
            self.live = {}

        def axes(self, u, h):
            if u == 3:
                return (yh * 2 + Y, yring) + ((x, xpeers, zpeers) if h == 0 else (z, zpeers, xpeers))
            return ((x, xpeers, z, zpeers) if h == 0 else (z, zpeers, x, xpeers)) + (ypeers,)

        def own(self, j):
            return pl.ds(mult(j * self.part, self.part), self.part)

        def a_start(self, u, h):
            i, peers, _, _, _ = self.axes(u, h)
            if ("a", u) not in self.live:
                self.live["a", u] = Group(self.RA.at[u], self.name + "a", self.RA)
            for k in (1, 2, 3):
                src = self.GP.at[u, :, h * 4 + (i + k) % 4]
                self.live["a", u].send(src, self.RA.at[u, h, k - 1], peers[k - 1])

        def a_finish(self, u):
            self.live["a", u].arrive()
            group = self.live["b", u] = Group(self.RB.at[u], self.name + "b", self.RB)
            for h in range(2):
                i, _, j, peers, _ = self.axes(u, h)
                total = self.GF[u, :, h * 4 + i]
                for k in range(3):
                    total = total + self.RA[u, h, k].astype(F32)
                self.CF[u, h] = total
                self.CB[u, h] = total.astype(BF)
                for k in (1, 2, 3):
                    src = self.CB.at[u, h, :, self.own((j + k) % 4), :]
                    group.send(src, self.RB.at[u, h, k - 1], peers[k - 1])

        def b_finish(self, u, s):
            self.live["b", u].arrive()
            for h in range(2):
                _, _, j, _, _ = self.axes(u, h)
                total = self.CF[u, h, :, self.own(j), :]
                for k in range(3):
                    total = total + self.RB[u, h, k].astype(F32)
                self.PF[s, h] = total
                self.PB[s, h] = total.astype(BF)

        def y_start(self, s):
            group = self.live["y", s] = Group(self.RY.at[s], self.name + "y", self.RY)
            for h in range(2):
                peers = ypeers if self.split else self.axes(s, h)[4]
                for k in range(3):
                    group.send(self.PB.at[s, h], self.RY.at[s, h, k], peers[k])

        def y_finish(self, s):
            self.live["y", s].arrive()
            group = self.live["gb", s] = Group(self.gb_ruler, self.name + "gb", self.gb_total)
            for h in range(2):
                i, _, j, peers, _ = self.axes(s, h)
                at = self.own(j)
                got = [self.RY[s, h, k].astype(F32) for k in range(3)]
                own = self.PF[s, h]
                if self.split:
                    self.G[s, Y, h * 4 + i, at, :] = (own + got[1])[0].astype(BF)
                    self.G[s, oY, h * 4 + i, at, :] = (got[0] + got[2])[0].astype(BF)
                else:
                    self.G[s, :, h * 4 + i, at, :] = (own + got[0] + (got[1] + got[2])).astype(BF)
                place = self.G.at[s, :, h * 4 + i, at, :]
                for to in peers:
                    group.send(place, place, to)

        def gb_finish(self, s):
            self.live["gb", s].arrive()
            group = self.live["ga", s] = Group(self.ga_ruler, self.name + "ga", RA2)
            for h in range(2):
                i, peers, _, _, _ = self.axes(s, h)
                place = self.G.at[s, :, h * 4 + i]
                for to in peers:
                    group.send(place, place, to)

        def ga_finish(self, s):
            self.live["ga", s].arrive()

    first = Reduce(
        "f", (GF1, GP1, RA1, CB1, CF1, RB1, PB1, PF1, RY1, G1), True, RA1.at[0, 0], RA1.at[0], RA1
    )
    second = Reduce(
        "s", (GF2, GP2, RA2, CB2, CF2, RB2, PB2, PF2, RY2, G2), False, RB2.at[0], RB2, RA2.at[0]
    )

    def left(start, n, lanes):
        return WB[0, pl.ds(start, n), :, :, :, lanes].reshape(n * 128, -1)

    def right(s, lanes):
        return WB[1, 2 * s + c, :, :, :, lanes].reshape(128, -1)

    def middle(it, i, order, inner_of):
        def body(n, _):
            lanes = pl.ds(mult(n * 512, 512), 512)
            inner = jnp.dot(inner_of, left(0, 4, lanes), preferred_element_type=F32)
            total = jnp.sum(inner[:128] * right(order[0], lanes).astype(F32), axis=0, keepdims=True)
            total = total + jnp.sum(
                inner[128:] * right(order[1], lanes).astype(F32), axis=0, keepdims=True
            )
            MID[it, 0, i:i + 1, lanes] = total
            return 0

        lax.fori_loop(0, 3, body, 0)

    def share(it):
        return one(MID.at[it, 0], MID.at[it, 1], core, "mid", MID.at[0])

    def ladder_weights(it, group):
        group.arrive()
        for i in range(2):
            for n in range(3):
                lanes = pl.ds(n * 512, 512)
                mid = MID[it, 0, i:i + 1, lanes] + MID[it, 1, i:i + 1, lanes]
                for k in range(2):
                    wr = right(blocks[k], lanes).astype(F32) * mid
                    WR[i, k * 128:(k + 1) * 128, lanes] = wr.astype(BF)

    def ladder(start, stop):
        def body(n, _):
            lf = left(n % 2 * 2, 2, pl.ds(0, 1536))
            LAD[pl.ds(mult(n * 256, 256), 256), :] = lax.dot_general(
                lf, WR[n // 2], NT, preferred_element_type=F32
            )
            return 0

        lax.fori_loop(start, stop, body, 0)

    def cycle(G, n, stages):
        here = pl.ds(mult(n * 256, 256), 256)
        mine = pl.ds(mult(Y * 1024 + n * 256, 256), 256)
        total = None
        for src, at, yy in ((BQ, mine, Y), (BR, here, oY)):
            for cc in range(2):
                weight = jnp.concatenate(
                    [
                        jnp.concatenate([G[s, yy, cc * 4 + q] for q in range(4)], axis=1)
                        for s in stages
                    ],
                    axis=0,
                )
                term = lax.dot_general(src[cc, at, :], weight, NT, preferred_element_type=F32)
                total = term if total is None else total + term
        return here, total

    def finish(n, here, k, total):
        va = VA[pl.ds(mult(n % 2 * 256, 256), 256), :]
        vb = vir[0:1, pl.ds(mult((2 * blocks[k] + c) * 128, 128), 128)]
        denom = va + vb - occ[2 * Y + n // 2] - piv[0]
        lad = LAD[here, k * 128:(k + 1) * 128]
        return ((C[k, here, :].astype(F32) + (total + lad)) / denom).astype(BF)

    b_in.arrive()
    gram1(0, Y, oc, 0)
    gram1(0, Y, oc, 1)
    for copy in lcopies[2:6] + lcopies[7:]:
        copy.wait()
    thc_y.arrive()
    wide = WB.at[0, 0, :, pl.ds(0, 3), :, pl.ds(0, 768)]
    lx = to_all(WB.at[0, z, :, x, :, plane], WB.at[0, z, :, x, :, plane], xpeers, wide, "near", WB.at[0, 0, :, pl.ds(0, 3)])
    rz = to_all(WB.at[1, z, :, x, :, plane], WB.at[1, z, :, x, :, plane], zpeers, wide, "near")
    for h in range(2):
        first.a_start(0, h)
    lx.arrive()
    rz.arrive()
    third = WB.at[0, pl.ds(0, 3), :, :, :, pl.ds(0, 384)]

    def spread(part, pair):
        lanes = pl.ds(mult(c * 768 + part * 384, 128), 384)
        for to in range(3):
            src = WB.at[0, z, :, :, :, lanes]
            pair[0].send(src, src, zpeers[to])
            src = WB.at[1, :, :, x, :, lanes]
            pair[1].send(src, src, xpeers[to])

    soon = [Group(third, "far", WB.at[0, pl.ds(0, 3)]), Group(third, "far")]
    spread(0, soon)
    first.a_finish(0)
    for half in range(2):
        t_in[half].arrive()
        transpose0(oY, half)
        gram1(1, oY, 0, half)
        if half == 0:
            move(0, EARLY)
        else:
            first.a_start(1, 0)
        gram1(1, oY, 1, half)
    first.a_start(1, 1)
    late = [Group(third, "far"), Group(third, "far")]
    spread(1, late)
    first.b_finish(0, (Y + c) % 2)
    first.a_finish(1)
    first.b_finish(1, (oY + c) % 2)
    for k in range(2):
        first.y_start(k)

    @pl.when(c == 0)
    def _():
        move(EARLY, N_MOVE)

    for group in soon + late:
        group.arrive()
    whole = WB.at[0, :, :, :, :, plane]
    thc_core = [one(whole, whole, core, "core", WB.at[0, pl.ds(0, 3)])]
    group = Group(WB.at[1, pl.ds(0, 2), :, :, :, pl.ds(0, 768)], "core")
    for k in range(2):
        place = WB.at[1, oc + 2 * k, :, :, :, plane]
        group.send(place, place, core)
    thc_core.append(group)
    for k in range(2):
        first.y_finish(k)
    for k in range(2):
        first.gb_finish(k)

    @pl.when(c == 1)
    def _():
        move(EARLY, N_MOVE)

    for group in thc_core:
        group.arrive()
    MID[0, 0] = jnp.zeros((8, 1536), F32)
    MID[1, 0] = jnp.zeros((8, 1536), F32)
    for i in range(2):
        at = pl.ds(mult(rows + i * 512, 512), 512)
        middle(0, i, (0, 1), TT0[:, :, at].reshape(256, 512))
    mid = share(0)
    forward(2)
    ladder_weights(0, mid)
    ladder(0, 4)
    forward(2)
    for k in range(2):
        first.ga_finish(k)

    def update1(n):
        here, total = cycle(G1, n, (0, 1))
        for k in range(2):
            value = finish(n, here, k, total[:, k * 128:(k + 1) * 128])
            TT1[k, :, here] = jnp.transpose(value)

    def first_rows(n, _):
        update1(n)
        return 0

    for group in forwarded:
        group.arrive()
    lax.fori_loop(0, 4, first_rows, 0)

    def gram2(cc):
        for src, at, yy in ((BQ, pl.ds(rows, 1024), Y), (BR, pl.ds(0, 1024), oY)):
            got = jnp.dot(
                TT1[...].reshape(256, 1024), src[cc, at, :], preferred_element_type=F32
            )
            for j in range(4):
                for q in range(4):
                    value = got[j * 64:(j + 1) * 64, q * 128:(q + 1) * 128]
                    GF2[j, yy, cc * 4 + q] = value
                    GP2[j, yy, cc * 4 + q] = value.astype(BF)
        for j in range(4):
            second.a_start(j, cc)

    gram2(0)
    gram2(1)

    for i in range(2):
        middle(1, i, blocks, TT1[:, :, i * 512:(i + 1) * 512].reshape(256, 512))
    mid = share(1)
    steps = [
        ("a", 0), ("a", 1), ("a", 2), ("a", 3), ("b", 0), ("b", 1), ("b", 2), ("b", 3),
        ("y", 0), ("y", 1), ("y", 2), ("y", 3), ("g", 0), ("g", 1), ("g", 2), ("g", 3), ("l", 0),
    ]
    for step, j in steps:
        if step == "l":
            ladder_weights(1, mid)
            ladder(0, 4)
        elif step == "a":
            second.a_finish(j)
        elif step == "b":
            second.b_finish(j, j)
            second.y_start(j)
        elif step == "y":
            second.y_finish(j)
        else:
            second.gb_finish(j)

    last = Group(TS)
    for k in range(2):
        second.ga_finish(2 * k)
        second.ga_finish(2 * k + 1)
        for n in range(4):
            here, total = cycle(G2, n, (2 * k, 2 * k + 1))
            value = finish(n, here, k, total)
            there = out.at[pl.ds(mult(Y * 1024 + n * 256, 256), 256), :]

            @pl.when(blocks[k] == oY)
            def _():
                TS[here, :] = value
                last.send(TS.at[here, :], there, ypeers[0])

            @pl.when(blocks[k] == Y)
            def _():
                T1[here, :] = value
                pltpu.make_async_copy(T1.at[here, :], there, ls.at[9]).start()

    pltpu.make_async_copy(T1, out.at[pl.ds(rows, 1024), :], ls.at[9]).wait()
    last.arrive()
    for m, total in kinds.values():
        pltpu.make_async_copy(total, total, ss.at[m]).wait()


def per_device(amplitudes, coulomb, df_factors, thc_left, thc_right, occ, vir, pivot):
    any_ = pl.BlockSpec(memory_space=pl.ANY)

    def reduce_scratch(n, m, b):
        return [
            pltpu.VMEM((n, m, 8, b, 128), F32),
            pltpu.VMEM((n, m, 8, b, 128), BF),
            pltpu.VMEM((n, 2, 3, m, b, 128), BF),
            pltpu.VMEM((n, 2, m, b, 128), BF),
            pltpu.VMEM((n, 2, m, b, 128), F32),
            pltpu.VMEM((n, 2, 3, m, b // 4, 128), BF),
            pltpu.VMEM((n, 2, m, b // 4, 128), BF),
            pltpu.VMEM((n, 2, m, b // 4, 128), F32),
            pltpu.VMEM((n, 2, 3, m, b // 4, 128), BF),
            pltpu.VMEM((n, 2, 8, b, 128), BF),
        ]

    return pl.pallas_call(
        kernel,
        out_shape=jax.ShapeDtypeStruct((2048, 128), BF),
        in_specs=[any_] * 8,
        out_specs=any_,
        scratch_shapes=[
            pltpu.VMEM((2, 2048, 512), BF),
            pltpu.VMEM((2, 1024, 512), BF),
            pltpu.VMEM((2, 2048, 128), BF),
            pltpu.VMEM((2, 128, 2048), BF),
            pltpu.VMEM((2, 128, 1024), BF),
            pltpu.VMEM((1024, 128), BF),
            pltpu.VMEM((1024, 128), BF),
            pltpu.VMEM((2, 1024, 128), BF),
            pltpu.VMEM((1024, 256), F32),
            pltpu.VMEM((512, 128), F32),
            pltpu.VMEM((2, 4, 2, 4, 16, 1536), BF),
            pltpu.VMEM((2, 256, 1536), BF),
            pltpu.VMEM((2, 2, 8, 1536), F32),
        ]
        + reduce_scratch(2, 1, 128)
        + reduce_scratch(4, 2, 64)
        + [
            pltpu.SemaphoreType.DMA((N_SENT,)),
            pltpu.SemaphoreType.DMA((N_SEM,)),
            pltpu.SemaphoreType.DMA((10,)),
            pltpu.SMEM((4,), F32),
            pltpu.VMEM((1, 512), F32),
            pltpu.SMEM((1,), F32),
        ],
        compiler_params=pltpu.CompilerParams(
            collective_id=0, has_side_effects=True, vmem_limit_bytes=56 * 2**20
        ),
    )(amplitudes, coulomb, df_factors, thc_left, thc_right, occ, vir.reshape(1, 512), pivot)


def solution(mesh):
    in_specs = (
        P("pair", "aux"),
        P("pair", None),
        P("pair", "aux"),
        P("pair", "aux"),
        P("pair", "aux"),
        P("pair"),
        P(),
        P(),
    )
    return jax.shard_map(
        per_device, mesh=mesh, in_specs=in_specs, out_specs=P("pair", "aux"), check_vma=False
    )
```

```python
import jax
import jax.numpy as jnp
from jax import lax
from jax.experimental import pallas as pl
from jax.experimental.pallas import tpu as pltpu
from jax.sharding import PartitionSpec as P

MESH = pl.DeviceIdType.MESH
BF = jnp.bfloat16
F32 = jnp.float32
N_SEM = 57
N_SENT = 20
N_MOVE = 8
EARLY = 4
NT = (((1,), (1,)), ((), ()))


def mult(value, n):
    return pl.multiple_of(value, n)


def kernel(
    amps, coul, df, tl, tr, occ_in, vir_in, piv_in, out,
    BQ, BR, T0, TT0, TT1, T1, TS, C, LAD, VA, WB, WR, MID,
    GF1, GP1, RA1, CB1, CF1, RB1, PB1, PF1, RY1, G1,
    GF2, GP2, RA2, CB2, CF2, RB2, PB2, PF2, RY2, G2,
    ss, rs, ls, occ, vir, piv,
):
    a = lax.axis_index("aux")
    p = lax.axis_index("pair")
    Y, c = a // 2, a % 2
    z, yh, x = p // 8, (p // 4) % 2, p % 4
    oY, oc, oyh = 1 - Y, 1 - c, 1 - yh

    def dev(Y=Y, c=c, z=z, yh=yh, x=x):
        return {"aux": Y * 2 + c, "pair": z * 8 + yh * 4 + x}

    ypeers = [dev(Y=oY), dev(yh=oyh), dev(Y=oY, yh=oyh)]
    yring = [dev(Y=(yh * 2 + Y + k) % 2, yh=(yh * 2 + Y + k) % 4 // 2) for k in (1, 2, 3)]
    xpeers = [dev(x=(x + k) % 4) for k in (1, 2, 3)]
    zpeers = [dev(z=(z + k) % 4) for k in (1, 2, 3)]
    core = dev(c=oc)
    blocks = [c, 1 - c]
    rows = mult(Y * 1024, 1024)
    orows = mult(oY * 1024, 1024)

    count = [0]
    kinds = {}

    class Group:
        def __init__(self, ruler, kind=None, total=None):
            self.n, self.ruler = count[0], ruler
            count[0] += 1
            if kind not in kinds:
                kind = kind or str(self.n)
                kinds[kind] = len(kinds), ruler if total is None else total
            self.m = kinds[kind][0]
            assert self.n < N_SEM and self.m < N_SENT

        def send(self, src, dst, to):
            pltpu.make_async_remote_copy(
                src_ref=src, dst_ref=dst, send_sem=ss.at[self.m], recv_sem=rs.at[self.n],
                device_id=to, device_id_type=MESH,
            ).start()

        def arrive(self):
            pltpu.make_async_copy(self.ruler, self.ruler, rs.at[self.n]).wait()

    def one(src, dst, to, *kind):
        group = Group(dst, *kind)
        group.send(src, dst, to)
        return group

    def to_all(src, dst, peers, ruler, *kind):
        group = Group(ruler, *kind)
        for to in peers:
            group.send(src, dst, to)
        return group

    piece = pl.ds(mult(c * 768 + Y * 384, 128), 384)
    plane = pl.ds(mult(c * 768, 128), 768)
    lcopies = []
    for n, (src, dst) in enumerate([
        (amps, T0.at[Y]),
        (df, BQ.at[c]),
        (tl, WB.at[0, z, yh, x, :, piece]),
        (tr, WB.at[1, z, yh, x, :, piece]),
        (coul.at[pl.ds(rows, 1024), pl.ds(mult((2 * blocks[0] + c) * 128, 128), 128)], C.at[0]),
        (coul.at[pl.ds(rows, 1024), pl.ds(mult((2 * blocks[1] + c) * 128, 128), 128)], C.at[1]),
        (vir_in, vir),
        (occ_in, occ),
        (piv_in, piv),
    ]):
        copy = pltpu.make_async_copy(src, dst, ls.at[n])
        copy.start()
        lcopies.append(copy)

    barrier = pltpu.get_barrier_semaphore()
    for to in ypeers + xpeers + zpeers + [core]:
        pl.semaphore_signal(barrier, inc=1, device_id=to, device_id_type=MESH)

    def transpose0(s, half):
        for n in range(2):
            at = pl.ds(half * 1024 + n * 512, 512)
            TT0[s, :, at] = jnp.transpose(T0[s, at, :])

    def gram1(f, s, cc, half):
        at = pl.ds(half * 1024, 1024)
        got = jnp.dot(TT0[s, :, at], BQ[cc, at, :], preferred_element_type=F32)
        for q in range(4):
            value = got[:, q * 128:(q + 1) * 128]
            if half == 1:
                value = GF1[f, 0, cc * 4 + q] + value
                GP1[f, 0, cc * 4 + q] = value.astype(BF)
            GF1[f, 0, cc * 4 + q] = value

    pl.semaphore_wait(barrier, 10)

    b_in = one(df, BQ.at[c], core)
    thc_y = Group(WB.at[0, 0, 0, pl.ds(0, 2), :, pl.ds(0, 1152)])
    for to in ypeers:
        thc_y.send(tl, WB.at[0, z, yh, x, :, piece], to)
        thc_y.send(tr, WB.at[1, z, yh, x, :, piece], to)
    t_in = []
    for half in range(2):
        at = pl.ds(half * 1024, 1024)
        t_in.append(one(amps.at[at, :], T0.at[Y, at, :], ypeers[0], "t", T0.at[0]))

    lcopies[0].wait()
    transpose0(Y, 0)
    transpose0(Y, 1)
    lcopies[6].wait()
    for q in range(4):
        row = vir[0:1, q * 128:(q + 1) * 128]
        VA[q * 128:(q + 1) * 128, :] = jnp.transpose(jnp.broadcast_to(row, (128, 128)))
    lcopies[1].wait()
    gram1(0, Y, c, 0)
    gram1(0, Y, c, 1)

    size = 1024 // N_MOVE
    moved = [Group(BR.at[0, pl.ds(n * size, size), :], "move", BR.at[0]) for n in range(N_MOVE)]

    def move(start, stop):
        for n in range(start, stop):
            src = df.at[pl.ds(mult(oY * 1024 + n * size, size), size), :]
            moved[n].send(src, BR.at[c, pl.ds(n * size, size), :], ypeers[0])

    forwarded = []

    def forward(count):
        start = len(forwarded) * 2
        for n in range(start, start + count * 2, 2):
            moved[n].arrive()
            moved[n + 1].arrive()
            block = BR.at[c, pl.ds(n * size, 2 * size), :]
            forwarded.append(one(block, block, core, "forward", BR.at[0]))

    class Reduce:
        def __init__(self, name, refs, split, gb_ruler, gb_total, ga_ruler):
            self.name, self.gb_total = name, gb_total
            self.GF, self.GP, self.RA, self.CB, self.CF = refs[:5]
            self.RB, self.PB, self.PF, self.RY, self.G = refs[5:]
            self.split, self.gb_ruler, self.ga_ruler = split, gb_ruler, ga_ruler
            self.part = self.GP.shape[3] // 4
            self.live = {}

        def axes(self, u, h):
            if u == 3:
                return (yh * 2 + Y, yring) + ((x, xpeers, zpeers) if h == 0 else (z, zpeers, xpeers))
            return ((x, xpeers, z, zpeers) if h == 0 else (z, zpeers, x, xpeers)) + (ypeers,)

        def own(self, j):
            return pl.ds(mult(j * self.part, self.part), self.part)

        def a_start(self, u, h):
            i, peers, _, _, _ = self.axes(u, h)
            if ("a", u) not in self.live:
                self.live["a", u] = Group(self.RA.at[u], self.name + "a", self.RA)
            for k in (1, 2, 3):
                src = self.GP.at[u, :, h * 4 + (i + k) % 4]
                self.live["a", u].send(src, self.RA.at[u, h, k - 1], peers[k - 1])

        def a_finish(self, u):
            self.live["a", u].arrive()
            group = self.live["b", u] = Group(self.RB.at[u], self.name + "b", self.RB)
            for h in range(2):
                i, _, j, peers, _ = self.axes(u, h)
                total = self.GF[u, :, h * 4 + i]
                for k in range(3):
                    total = total + self.RA[u, h, k].astype(F32)
                self.CF[u, h] = total
                self.CB[u, h] = total.astype(BF)
                for k in (1, 2, 3):
                    src = self.CB.at[u, h, :, self.own((j + k) % 4), :]
                    group.send(src, self.RB.at[u, h, k - 1], peers[k - 1])

        def b_finish(self, u, s):
            self.live["b", u].arrive()
            for h in range(2):
                _, _, j, _, _ = self.axes(u, h)
                total = self.CF[u, h, :, self.own(j), :]
                for k in range(3):
                    total = total + self.RB[u, h, k].astype(F32)
                self.PF[s, h] = total
                self.PB[s, h] = total.astype(BF)

        def y_start(self, s):
            group = self.live["y", s] = Group(self.RY.at[s], self.name + "y", self.RY)
            for h in range(2):
                peers = ypeers if self.split else self.axes(s, h)[4]
                for k in range(3):
                    group.send(self.PB.at[s, h], self.RY.at[s, h, k], peers[k])

        def y_finish(self, s):
            self.live["y", s].arrive()
            group = self.live["gb", s] = Group(self.gb_ruler, self.name + "gb", self.gb_total)
            for h in range(2):
                i, _, j, peers, _ = self.axes(s, h)
                at = self.own(j)
                got = [self.RY[s, h, k].astype(F32) for k in range(3)]
                own = self.PF[s, h]
                if self.split:
                    self.G[s, Y, h * 4 + i, at, :] = (own + got[1])[0].astype(BF)
                    self.G[s, oY, h * 4 + i, at, :] = (got[0] + got[2])[0].astype(BF)
                else:
                    self.G[s, :, h * 4 + i, at, :] = (own + got[0] + (got[1] + got[2])).astype(BF)
                place = self.G.at[s, :, h * 4 + i, at, :]
                for to in peers:
                    group.send(place, place, to)

        def gb_finish(self, s):
            self.live["gb", s].arrive()
            group = self.live["ga", s] = Group(self.ga_ruler, self.name + "ga", RA2)
            for h in range(2):
                i, peers, _, _, _ = self.axes(s, h)
                place = self.G.at[s, :, h * 4 + i]
                for to in peers:
                    group.send(place, place, to)

        def ga_finish(self, s):
            self.live["ga", s].arrive()

    first = Reduce(
        "f", (GF1, GP1, RA1, CB1, CF1, RB1, PB1, PF1, RY1, G1), True, RA1.at[0, 0], RA1.at[0], RA1
    )
    second = Reduce(
        "s", (GF2, GP2, RA2, CB2, CF2, RB2, PB2, PF2, RY2, G2), False, RB2.at[0], RB2, RA2.at[0]
    )

    def left(start, n, lanes):
        return WB[0, pl.ds(start, n), :, :, :, lanes].reshape(n * 128, -1)

    def right(s, lanes):
        return WB[1, 2 * s + c, :, :, :, lanes].reshape(128, -1)

    def middle(it, i, order, inner_of):
        def body(n, _):
            lanes = pl.ds(mult(n * 512, 512), 512)
            inner = jnp.dot(inner_of, left(0, 4, lanes), preferred_element_type=F32)
            total = jnp.sum(inner[:128] * right(order[0], lanes).astype(F32), axis=0, keepdims=True)
            total = total + jnp.sum(
                inner[128:] * right(order[1], lanes).astype(F32), axis=0, keepdims=True
            )
            MID[it, 0, i:i + 1, lanes] = total
            return 0

        lax.fori_loop(0, 3, body, 0)

    def share(it):
        return one(MID.at[it, 0], MID.at[it, 1], core, "mid", MID.at[0])

    def ladder_weights(it, group):
        group.arrive()
        for i in range(2):
            for n in range(3):
                lanes = pl.ds(n * 512, 512)
                mid = MID[it, 0, i:i + 1, lanes] + MID[it, 1, i:i + 1, lanes]
                for k in range(2):
                    wr = right(blocks[k], lanes).astype(F32) * mid
                    WR[i, k * 128:(k + 1) * 128, lanes] = wr.astype(BF)

    def ladder(start, stop):
        def body(n, _):
            lf = left(n % 2 * 2, 2, pl.ds(0, 1536))
            LAD[pl.ds(mult(n * 256, 256), 256), :] = lax.dot_general(
                lf, WR[n // 2], NT, preferred_element_type=F32
            )
            return 0

        lax.fori_loop(start, stop, body, 0)

    def cycle(G, n, stages, size=256):
        here = pl.ds(mult(n * size, size), size)
        mine = pl.ds(mult(Y * 1024 + n * size, size), size)
        total = None
        for src, at, yy in ((BQ, mine, Y), (BR, here, oY)):
            for cc in range(2):
                weight = jnp.concatenate(
                    [
                        jnp.concatenate([G[s, yy, cc * 4 + q] for q in range(4)], axis=1)
                        for s in stages
                    ],
                    axis=0,
                )
                term = lax.dot_general(src[cc, at, :], weight, NT, preferred_element_type=F32)
                total = term if total is None else total + term
        return here, total

    def finish(n, here, k, total, size=256):
        per = 512 // size
        va = VA[pl.ds(mult(n % per * size, size), size), :]
        vb = vir[0:1, pl.ds(mult((2 * blocks[k] + c) * 128, 128), 128)]
        denom = va + vb - occ[2 * Y + n // per] - piv[0]
        lad = LAD[here, k * 128:(k + 1) * 128]
        return ((C[k, here, :].astype(F32) + (total + lad)) / denom).astype(BF)

    b_in.arrive()
    gram1(0, Y, oc, 0)
    gram1(0, Y, oc, 1)
    for copy in lcopies[2:6] + lcopies[7:]:
        copy.wait()
    thc_y.arrive()
    wide = WB.at[0, 0, :, pl.ds(0, 3), :, pl.ds(0, 768)]
    lx = to_all(WB.at[0, z, :, x, :, plane], WB.at[0, z, :, x, :, plane], xpeers, wide, "near", WB.at[0, 0, :, pl.ds(0, 3)])
    rz = to_all(WB.at[1, z, :, x, :, plane], WB.at[1, z, :, x, :, plane], zpeers, wide, "near")
    for h in range(2):
        first.a_start(0, h)
    lx.arrive()
    rz.arrive()
    third = WB.at[0, pl.ds(0, 3), :, :, :, pl.ds(0, 384)]

    def spread(part, pair):
        lanes = pl.ds(mult(c * 768 + part * 384, 128), 384)
        for to in range(3):
            src = WB.at[0, z, :, :, :, lanes]
            pair[0].send(src, src, zpeers[to])
            src = WB.at[1, :, :, x, :, lanes]
            pair[1].send(src, src, xpeers[to])

    soon = [Group(third, "far", WB.at[0, pl.ds(0, 3)]), Group(third, "far")]
    spread(0, soon)
    first.a_finish(0)
    for half in range(2):
        t_in[half].arrive()
        transpose0(oY, half)
        gram1(1, oY, 0, half)
        if half == 0:
            move(0, EARLY)
        else:
            first.a_start(1, 0)
        gram1(1, oY, 1, half)
    first.a_start(1, 1)
    late = [Group(third, "far"), Group(third, "far")]
    spread(1, late)
    first.b_finish(0, (Y + c) % 2)
    first.a_finish(1)
    first.b_finish(1, (oY + c) % 2)
    for k in range(2):
        first.y_start(k)

    @pl.when(c == 0)
    def _():
        move(EARLY, N_MOVE)

    for group in soon + late:
        group.arrive()
    whole = WB.at[0, :, :, :, :, plane]
    thc_core = [one(whole, whole, core, "core", WB.at[0, pl.ds(0, 3)])]
    group = Group(WB.at[1, pl.ds(0, 2), :, :, :, pl.ds(0, 768)], "core")
    for k in range(2):
        place = WB.at[1, oc + 2 * k, :, :, :, plane]
        group.send(place, place, core)
    thc_core.append(group)
    for k in range(2):
        first.y_finish(k)
    for k in range(2):
        first.gb_finish(k)

    @pl.when(c == 1)
    def _():
        move(EARLY, N_MOVE)

    for group in thc_core:
        group.arrive()
    MID[0, 0] = jnp.zeros((8, 1536), F32)
    MID[1, 0] = jnp.zeros((8, 1536), F32)
    for i in range(2):
        at = pl.ds(mult(rows + i * 512, 512), 512)
        middle(0, i, (0, 1), TT0[:, :, at].reshape(256, 512))
    mid = share(0)
    forward(2)
    ladder_weights(0, mid)
    ladder(0, 4)
    forward(2)
    for k in range(2):
        first.ga_finish(k)

    def update1(n):
        here, total = cycle(G1, n, (0, 1), 512)
        for k in range(2):
            value = finish(n, here, k, total[:, k * 128:(k + 1) * 128], 512)
            TT1[k, :, here] = jnp.transpose(value)

    def first_rows(n, _):
        update1(n)
        return 0

    for group in forwarded:
        group.arrive()
    lax.fori_loop(0, 2, first_rows, 0)

    def gram2(cc):
        for src, at, yy in ((BQ, pl.ds(rows, 1024), Y), (BR, pl.ds(0, 1024), oY)):
            got = jnp.dot(
                TT1[...].reshape(256, 1024), src[cc, at, :], preferred_element_type=F32
            )
            for j in range(4):
                for q in range(4):
                    value = got[j * 64:(j + 1) * 64, q * 128:(q + 1) * 128]
                    GF2[j, yy, cc * 4 + q] = value
                    GP2[j, yy, cc * 4 + q] = value.astype(BF)
        for j in range(4):
            second.a_start(j, cc)

    gram2(0)
    gram2(1)

    for i in range(2):
        middle(1, i, blocks, TT1[:, :, i * 512:(i + 1) * 512].reshape(256, 512))
    mid = share(1)
    steps = [
        ("a", 0), ("a", 1), ("a", 2), ("a", 3), ("b", 0), ("b", 1), ("b", 2), ("b", 3),
        ("y", 0), ("y", 1), ("y", 2), ("y", 3), ("g", 0), ("g", 1), ("g", 2), ("g", 3), ("l", 0),
    ]
    for step, j in steps:
        if step == "l":
            ladder_weights(1, mid)
            ladder(0, 4)
        elif step == "a":
            second.a_finish(j)
        elif step == "b":
            second.b_finish(j, j)
            second.y_start(j)
        elif step == "y":
            second.y_finish(j)
        else:
            second.gb_finish(j)

    last = Group(TS)
    for k in range(2):
        second.ga_finish(2 * k)
        second.ga_finish(2 * k + 1)
        for n in range(8):
            here, total = cycle(G2, n, (2 * k, 2 * k + 1), 128)
            value = finish(n, here, k, total, 128)
            there = out.at[pl.ds(mult(Y * 1024 + n * 128, 128), 128), :]

            @pl.when(blocks[k] == oY)
            def _():
                TS[here, :] = value
                last.send(TS.at[here, :], there, ypeers[0])

            @pl.when(blocks[k] == Y)
            def _():
                T1[here, :] = value
                pltpu.make_async_copy(T1.at[here, :], there, ls.at[9]).start()

    pltpu.make_async_copy(T1, out.at[pl.ds(rows, 1024), :], ls.at[9]).wait()
    last.arrive()
    for m, total in kinds.values():
        pltpu.make_async_copy(total, total, ss.at[m]).wait()


def per_device(amplitudes, coulomb, df_factors, thc_left, thc_right, occ, vir, pivot):
    any_ = pl.BlockSpec(memory_space=pl.ANY)

    def reduce_scratch(n, m, b):
        return [
            pltpu.VMEM((n, m, 8, b, 128), F32),
            pltpu.VMEM((n, m, 8, b, 128), BF),
            pltpu.VMEM((n, 2, 3, m, b, 128), BF),
            pltpu.VMEM((n, 2, m, b, 128), BF),
            pltpu.VMEM((n, 2, m, b, 128), F32),
            pltpu.VMEM((n, 2, 3, m, b // 4, 128), BF),
            pltpu.VMEM((n, 2, m, b // 4, 128), BF),
            pltpu.VMEM((n, 2, m, b // 4, 128), F32),
            pltpu.VMEM((n, 2, 3, m, b // 4, 128), BF),
            pltpu.VMEM((n, 2, 8, b, 128), BF),
        ]

    return pl.pallas_call(
        kernel,
        out_shape=jax.ShapeDtypeStruct((2048, 128), BF),
        in_specs=[any_] * 8,
        out_specs=any_,
        scratch_shapes=[
            pltpu.VMEM((2, 2048, 512), BF),
            pltpu.VMEM((2, 1024, 512), BF),
            pltpu.VMEM((2, 2048, 128), BF),
            pltpu.VMEM((2, 128, 2048), BF),
            pltpu.VMEM((2, 128, 1024), BF),
            pltpu.VMEM((1024, 128), BF),
            pltpu.VMEM((1024, 128), BF),
            pltpu.VMEM((2, 1024, 128), BF),
            pltpu.VMEM((1024, 256), F32),
            pltpu.VMEM((512, 128), F32),
            pltpu.VMEM((2, 4, 2, 4, 16, 1536), BF),
            pltpu.VMEM((2, 256, 1536), BF),
            pltpu.VMEM((2, 2, 8, 1536), F32),
        ]
        + reduce_scratch(2, 1, 128)
        + reduce_scratch(4, 2, 64)
        + [
            pltpu.SemaphoreType.DMA((N_SENT,)),
            pltpu.SemaphoreType.DMA((N_SEM,)),
            pltpu.SemaphoreType.DMA((10,)),
            pltpu.SMEM((4,), F32),
            pltpu.VMEM((1, 512), F32),
            pltpu.SMEM((1,), F32),
        ],
        compiler_params=pltpu.CompilerParams(
            collective_id=0, has_side_effects=True, vmem_limit_bytes=56 * 2**20
        ),
    )(amplitudes, coulomb, df_factors, thc_left, thc_right, occ, vir.reshape(1, 512), pivot)


def solution(mesh):
    in_specs = (
        P("pair", "aux"),
        P("pair", None),
        P("pair", "aux"),
        P("pair", "aux"),
        P("pair", "aux"),
        P("pair"),
        P(),
        P(),
    )
    return jax.shard_map(
        per_device, mesh=mesh, in_specs=in_specs, out_specs=P("pair", "aux"), check_vma=False
    )
```

```python
import jax
import jax.numpy as jnp
from jax import lax
from jax.experimental import pallas as pl
from jax.experimental.pallas import tpu as pltpu
from jax.sharding import PartitionSpec as P

MESH = pl.DeviceIdType.MESH
BF = jnp.bfloat16
F32 = jnp.float32
N_SEM = 57
N_SENT = 20
N_MOVE = 8
EARLY = 4
NT = (((1,), (1,)), ((), ()))


def mult(value, n):
    return pl.multiple_of(value, n)


def kernel(
    amps, coul, df, tl, tr, occ_in, vir_in, piv_in, out,
    BQ, BR, T0, TT0, TT1, T1, TS, C, LAD, VA, WB, WR, MID,
    GF1, GP1, RA1, CB1, CF1, RB1, PB1, PF1, RY1, G1,
    GF2, GP2, RA2, CB2, CF2, RB2, PB2, PF2, RY2, G2,
    ss, rs, ls, occ, vir, piv,
):
    a = lax.axis_index("aux")
    p = lax.axis_index("pair")
    Y, c = a // 2, a % 2
    z, yh, x = p // 8, (p // 4) % 2, p % 4
    oY, oc, oyh = 1 - Y, 1 - c, 1 - yh

    def dev(Y=Y, c=c, z=z, yh=yh, x=x):
        return {"aux": Y * 2 + c, "pair": z * 8 + yh * 4 + x}

    ypeers = [dev(Y=oY), dev(yh=oyh), dev(Y=oY, yh=oyh)]
    yring = [dev(Y=(yh * 2 + Y + k) % 2, yh=(yh * 2 + Y + k) % 4 // 2) for k in (1, 2, 3)]
    xpeers = [dev(x=(x + k) % 4) for k in (1, 2, 3)]
    zpeers = [dev(z=(z + k) % 4) for k in (1, 2, 3)]
    core = dev(c=oc)
    blocks = [c, 1 - c]
    rows = mult(Y * 1024, 1024)
    orows = mult(oY * 1024, 1024)

    count = [0]
    kinds = {}

    class Group:
        def __init__(self, ruler, kind=None, total=None):
            self.n, self.ruler = count[0], ruler
            count[0] += 1
            if kind not in kinds:
                kind = kind or str(self.n)
                kinds[kind] = len(kinds), ruler if total is None else total
            self.m = kinds[kind][0]
            assert self.n < N_SEM and self.m < N_SENT

        def send(self, src, dst, to):
            pltpu.make_async_remote_copy(
                src_ref=src, dst_ref=dst, send_sem=ss.at[self.m], recv_sem=rs.at[self.n],
                device_id=to, device_id_type=MESH,
            ).start()

        def arrive(self):
            pltpu.make_async_copy(self.ruler, self.ruler, rs.at[self.n]).wait()

    def one(src, dst, to, *kind):
        group = Group(dst, *kind)
        group.send(src, dst, to)
        return group

    def to_all(src, dst, peers, ruler, *kind):
        group = Group(ruler, *kind)
        for to in peers:
            group.send(src, dst, to)
        return group

    piece = pl.ds(mult(c * 768 + Y * 384, 128), 384)
    plane = pl.ds(mult(c * 768, 128), 768)
    lcopies = []
    for n, (src, dst) in enumerate([
        (amps, T0.at[Y]),
        (df, BQ.at[c]),
        (tl, WB.at[0, z, yh, x, :, piece]),
        (tr, WB.at[1, z, yh, x, :, piece]),
        (coul.at[pl.ds(rows, 1024), pl.ds(mult((2 * blocks[0] + c) * 128, 128), 128)], C.at[0]),
        (coul.at[pl.ds(rows, 1024), pl.ds(mult((2 * blocks[1] + c) * 128, 128), 128)], C.at[1]),
        (vir_in, vir),
        (occ_in, occ),
        (piv_in, piv),
    ]):
        copy = pltpu.make_async_copy(src, dst, ls.at[n])
        copy.start()
        lcopies.append(copy)

    barrier = pltpu.get_barrier_semaphore()
    for to in ypeers + xpeers + zpeers + [core]:
        pl.semaphore_signal(barrier, inc=1, device_id=to, device_id_type=MESH)

    def transpose0(s, half):
        for n in range(2):
            at = pl.ds(half * 1024 + n * 512, 512)
            TT0[s, :, at] = jnp.transpose(T0[s, at, :])

    def gram1(f, s, cc, half):
        at = pl.ds(half * 1024, 1024)
        got = jnp.dot(TT0[s, :, at], BQ[cc, at, :], preferred_element_type=F32)
        for q in range(4):
            value = got[:, q * 128:(q + 1) * 128]
            if half == 1:
                value = GF1[f, 0, cc * 4 + q] + value
                GP1[f, 0, cc * 4 + q] = value.astype(BF)
            GF1[f, 0, cc * 4 + q] = value

    pl.semaphore_wait(barrier, 10)

    b_in = one(df, BQ.at[c], core)
    thc_y = Group(WB.at[0, 0, 0, pl.ds(0, 2), :, pl.ds(0, 1152)])
    for to in ypeers:
        thc_y.send(tl, WB.at[0, z, yh, x, :, piece], to)
        thc_y.send(tr, WB.at[1, z, yh, x, :, piece], to)
    t_in = []
    for half in range(2):
        at = pl.ds(half * 1024, 1024)
        t_in.append(one(amps.at[at, :], T0.at[Y, at, :], ypeers[0], "t", T0.at[0]))

    lcopies[0].wait()
    transpose0(Y, 0)
    transpose0(Y, 1)
    lcopies[6].wait()
    for q in range(4):
        row = vir[0:1, q * 128:(q + 1) * 128]
        VA[q * 128:(q + 1) * 128, :] = jnp.transpose(jnp.broadcast_to(row, (128, 128)))
    lcopies[1].wait()
    gram1(0, Y, c, 0)
    gram1(0, Y, c, 1)

    size = 1024 // N_MOVE
    moved = [Group(BR.at[0, pl.ds(n * size, size), :], "move", BR.at[0]) for n in range(N_MOVE)]

    def move(start, stop):
        for n in range(start, stop):
            src = df.at[pl.ds(mult(oY * 1024 + n * size, size), size), :]
            moved[n].send(src, BR.at[c, pl.ds(n * size, size), :], ypeers[0])

    forwarded = []

    def forward(count):
        start = len(forwarded) * 2
        for n in range(start, start + count * 2, 2):
            moved[n].arrive()
            moved[n + 1].arrive()
            block = BR.at[c, pl.ds(n * size, 2 * size), :]
            forwarded.append(one(block, block, core, "forward", BR.at[0]))

    class Reduce:
        def __init__(self, name, refs, split, gb_ruler, gb_total, ga_ruler):
            self.name, self.gb_total = name, gb_total
            self.GF, self.GP, self.RA, self.CB, self.CF = refs[:5]
            self.RB, self.PB, self.PF, self.RY, self.G = refs[5:]
            self.split, self.gb_ruler, self.ga_ruler = split, gb_ruler, ga_ruler
            self.part = self.GP.shape[3] // 4
            self.live = {}

        def axes(self, u, h):
            if u == 3:
                return (yh * 2 + Y, yring) + ((x, xpeers, zpeers) if h == 0 else (z, zpeers, xpeers))
            return ((x, xpeers, z, zpeers) if h == 0 else (z, zpeers, x, xpeers)) + (ypeers,)

        def own(self, j):
            return pl.ds(mult(j * self.part, self.part), self.part)

        def a_start(self, u, h):
            i, peers, _, _, _ = self.axes(u, h)
            if ("a", u) not in self.live:
                self.live["a", u] = Group(self.RA.at[u], self.name + "a", self.RA)
            for k in (1, 2, 3):
                src = self.GP.at[u, :, h * 4 + (i + k) % 4]
                self.live["a", u].send(src, self.RA.at[u, h, k - 1], peers[k - 1])

        def a_finish(self, u):
            self.live["a", u].arrive()
            group = self.live["b", u] = Group(self.RB.at[u], self.name + "b", self.RB)
            for h in range(2):
                i, _, j, peers, _ = self.axes(u, h)
                total = self.GF[u, :, h * 4 + i]
                for k in range(3):
                    total = total + self.RA[u, h, k].astype(F32)
                self.CF[u, h] = total
                self.CB[u, h] = total.astype(BF)
                for k in (1, 2, 3):
                    src = self.CB.at[u, h, :, self.own((j + k) % 4), :]
                    group.send(src, self.RB.at[u, h, k - 1], peers[k - 1])

        def b_finish(self, u, s):
            self.live["b", u].arrive()
            for h in range(2):
                _, _, j, _, _ = self.axes(u, h)
                total = self.CF[u, h, :, self.own(j), :]
                for k in range(3):
                    total = total + self.RB[u, h, k].astype(F32)
                self.PF[s, h] = total
                self.PB[s, h] = total.astype(BF)

        def y_start(self, s):
            group = self.live["y", s] = Group(self.RY.at[s], self.name + "y", self.RY)
            for h in range(2):
                peers = ypeers if self.split else self.axes(s, h)[4]
                for k in range(3):
                    group.send(self.PB.at[s, h], self.RY.at[s, h, k], peers[k])

        def y_finish(self, s):
            self.live["y", s].arrive()
            group = self.live["gb", s] = Group(self.gb_ruler, self.name + "gb", self.gb_total)
            for h in range(2):
                i, _, j, peers, _ = self.axes(s, h)
                at = self.own(j)
                got = [self.RY[s, h, k].astype(F32) for k in range(3)]
                own = self.PF[s, h]
                if self.split:
                    self.G[s, Y, h * 4 + i, at, :] = (own + got[1])[0].astype(BF)
                    self.G[s, oY, h * 4 + i, at, :] = (got[0] + got[2])[0].astype(BF)
                else:
                    self.G[s, :, h * 4 + i, at, :] = (own + got[0] + (got[1] + got[2])).astype(BF)
                place = self.G.at[s, :, h * 4 + i, at, :]
                for to in peers:
                    group.send(place, place, to)

        def gb_finish(self, s):
            self.live["gb", s].arrive()
            group = self.live["ga", s] = Group(self.ga_ruler, self.name + "ga", RA2)
            for h in range(2):
                i, peers, _, _, _ = self.axes(s, h)
                place = self.G.at[s, :, h * 4 + i]
                for to in peers:
                    group.send(place, place, to)

        def ga_finish(self, s):
            self.live["ga", s].arrive()

    first = Reduce(
        "f", (GF1, GP1, RA1, CB1, CF1, RB1, PB1, PF1, RY1, G1), True, RA1.at[0, 0], RA1.at[0], RA1
    )
    second = Reduce(
        "s", (GF2, GP2, RA2, CB2, CF2, RB2, PB2, PF2, RY2, G2), False, RB2.at[0], RB2, RA2.at[0]
    )

    def left(start, n, lanes):
        return WB[0, pl.ds(start, n), :, :, :, lanes].reshape(n * 128, -1)

    def right(s, lanes):
        return WB[1, 2 * s + c, :, :, :, lanes].reshape(128, -1)

    def middle(it, i, order, inner_of):
        def body(n, _):
            lanes = pl.ds(mult(n * 512, 512), 512)
            inner = jnp.dot(inner_of, left(0, 4, lanes), preferred_element_type=F32)
            total = jnp.sum(inner[:128] * right(order[0], lanes).astype(F32), axis=0, keepdims=True)
            total = total + jnp.sum(
                inner[128:] * right(order[1], lanes).astype(F32), axis=0, keepdims=True
            )
            MID[it, 0, i:i + 1, lanes] = total
            return 0

        lax.fori_loop(0, 3, body, 0)

    def share(it):
        return one(MID.at[it, 0], MID.at[it, 1], core, "mid", MID.at[0])

    def ladder_weights(it, group):
        group.arrive()
        for i in range(2):
            for n in range(3):
                lanes = pl.ds(n * 512, 512)
                mid = MID[it, 0, i:i + 1, lanes] + MID[it, 1, i:i + 1, lanes]
                for k in range(2):
                    wr = right(blocks[k], lanes).astype(F32) * mid
                    WR[i, k * 128:(k + 1) * 128, lanes] = wr.astype(BF)

    def ladder(start, stop):
        def body(n, _):
            lf = left(n % 2 * 2, 2, pl.ds(0, 1536))
            LAD[pl.ds(mult(n * 256, 256), 256), :] = lax.dot_general(
                lf, WR[n // 2], NT, preferred_element_type=F32
            )
            return 0

        lax.fori_loop(start, stop, body, 0)

    def cycle(G, n, stages, size=256):
        here = pl.ds(mult(n * size, size), size)
        mine = pl.ds(mult(Y * 1024 + n * size, size), size)
        total = None
        for src, at, yy in ((BQ, mine, Y), (BR, here, oY)):
            for cc in range(2):
                weight = jnp.concatenate(
                    [
                        jnp.concatenate([G[s, yy, cc * 4 + q] for q in range(4)], axis=1)
                        for s in stages
                    ],
                    axis=0,
                )
                term = lax.dot_general(src[cc, at, :], weight, NT, preferred_element_type=F32)
                total = term if total is None else total + term
        return here, total

    def finish(n, here, k, total, size=256):
        per = 512 // size
        va = VA[pl.ds(mult(n % per * size, size), size), :]
        vb = vir[0:1, pl.ds(mult((2 * blocks[k] + c) * 128, 128), 128)]
        denom = va + vb - occ[2 * Y + n // per] - piv[0]
        lad = LAD[here, k * 128:(k + 1) * 128]
        return ((C[k, here, :].astype(F32) + (total + lad)) / denom).astype(BF)

    b_in.arrive()
    gram1(0, Y, oc, 0)
    gram1(0, Y, oc, 1)
    for copy in lcopies[2:6] + lcopies[7:]:
        copy.wait()
    thc_y.arrive()
    wide = WB.at[0, 0, :, pl.ds(0, 3), :, pl.ds(0, 768)]
    lx = to_all(WB.at[0, z, :, x, :, plane], WB.at[0, z, :, x, :, plane], xpeers, wide, "near", WB.at[0, 0, :, pl.ds(0, 3)])
    rz = to_all(WB.at[1, z, :, x, :, plane], WB.at[1, z, :, x, :, plane], zpeers, wide, "near")
    for h in range(2):
        first.a_start(0, h)
    lx.arrive()
    rz.arrive()
    third = WB.at[0, pl.ds(0, 3), :, :, :, pl.ds(0, 384)]

    def spread(part, pair):
        lanes = pl.ds(mult(c * 768 + part * 384, 128), 384)
        for to in range(3):
            src = WB.at[0, z, :, :, :, lanes]
            pair[0].send(src, src, zpeers[to])
            src = WB.at[1, :, :, x, :, lanes]
            pair[1].send(src, src, xpeers[to])

    soon = [Group(third, "far", WB.at[0, pl.ds(0, 3)]), Group(third, "far")]
    spread(0, soon)
    first.a_finish(0)
    for half in range(2):
        t_in[half].arrive()
        transpose0(oY, half)
        gram1(1, oY, 0, half)
        if half == 0:
            move(0, EARLY)
        else:
            first.a_start(1, 0)
        gram1(1, oY, 1, half)
    first.a_start(1, 1)
    late = [Group(third, "far"), Group(third, "far")]
    spread(1, late)
    first.b_finish(0, (Y + c) % 2)
    first.a_finish(1)
    first.b_finish(1, (oY + c) % 2)
    for k in range(2):
        first.y_start(k)

    @pl.when(c == 0)
    def _():
        move(EARLY, N_MOVE)

    for group in soon + late:
        group.arrive()
    whole = WB.at[0, :, :, :, :, plane]
    thc_core = [one(whole, whole, core, "core", WB.at[0, pl.ds(0, 3)])]
    group = Group(WB.at[1, pl.ds(0, 2), :, :, :, pl.ds(0, 768)], "core")
    for k in range(2):
        place = WB.at[1, oc + 2 * k, :, :, :, plane]
        group.send(place, place, core)
    thc_core.append(group)
    for k in range(2):
        first.y_finish(k)
    for k in range(2):
        first.gb_finish(k)

    @pl.when(c == 1)
    def _():
        move(EARLY, N_MOVE)

    for group in thc_core:
        group.arrive()
    MID[0, 0] = jnp.zeros((8, 1536), F32)
    MID[1, 0] = jnp.zeros((8, 1536), F32)
    for i in range(2):
        at = pl.ds(mult(rows + i * 512, 512), 512)
        middle(0, i, (0, 1), TT0[:, :, at].reshape(256, 512))
    mid = share(0)
    forward(2)
    ladder_weights(0, mid)
    ladder(0, 4)
    forward(2)
    for k in range(2):
        first.ga_finish(k)

    def update1(n):
        here, total = cycle(G1, n, (0, 1), 512)
        for k in range(2):
            value = finish(n, here, k, total[:, k * 128:(k + 1) * 128], 512)
            TT1[k, :, here] = jnp.transpose(value)

    def first_rows(n, _):
        update1(n)
        return 0

    for n in range(2):
        for group in forwarded[2 * n:2 * n + 2]:
            group.arrive()
        lax.fori_loop(n, n + 1, first_rows, 0)

    def gram2(cc):
        for src, at, yy in ((BQ, pl.ds(rows, 1024), Y), (BR, pl.ds(0, 1024), oY)):
            got = jnp.dot(
                TT1[...].reshape(256, 1024), src[cc, at, :], preferred_element_type=F32
            )
            for j in range(4):
                for q in range(4):
                    value = got[j * 64:(j + 1) * 64, q * 128:(q + 1) * 128]
                    GF2[j, yy, cc * 4 + q] = value
                    GP2[j, yy, cc * 4 + q] = value.astype(BF)
        for j in range(4):
            second.a_start(j, cc)

    gram2(0)
    gram2(1)

    for i in range(2):
        middle(1, i, blocks, TT1[:, :, i * 512:(i + 1) * 512].reshape(256, 512))
    mid = share(1)
    steps = [
        ("a", 0), ("a", 1), ("a", 2), ("a", 3), ("b", 0), ("b", 1), ("b", 2), ("b", 3),
        ("y", 0), ("y", 1), ("y", 2), ("y", 3), ("g", 0), ("g", 1), ("g", 2), ("g", 3), ("l", 0),
    ]
    for step, j in steps:
        if step == "l":
            ladder_weights(1, mid)
            ladder(0, 4)
        elif step == "a":
            second.a_finish(j)
        elif step == "b":
            second.b_finish(j, j)
            second.y_start(j)
        elif step == "y":
            second.y_finish(j)
        else:
            second.gb_finish(j)

    last = Group(TS)
    for k in range(2):
        second.ga_finish(2 * k)
        second.ga_finish(2 * k + 1)
        for n in range(8):
            here, total = cycle(G2, n, (2 * k, 2 * k + 1), 128)
            value = finish(n, here, k, total, 128)
            there = out.at[pl.ds(mult(Y * 1024 + n * 128, 128), 128), :]

            @pl.when(blocks[k] == oY)
            def _():
                TS[here, :] = value
                last.send(TS.at[here, :], there, ypeers[0])

            @pl.when(blocks[k] == Y)
            def _():
                T1[here, :] = value
                pltpu.make_async_copy(T1.at[here, :], there, ls.at[9]).start()

    pltpu.make_async_copy(T1, out.at[pl.ds(rows, 1024), :], ls.at[9]).wait()
    last.arrive()
    for m, total in kinds.values():
        pltpu.make_async_copy(total, total, ss.at[m]).wait()


def per_device(amplitudes, coulomb, df_factors, thc_left, thc_right, occ, vir, pivot):
    any_ = pl.BlockSpec(memory_space=pl.ANY)

    def reduce_scratch(n, m, b):
        return [
            pltpu.VMEM((n, m, 8, b, 128), F32),
            pltpu.VMEM((n, m, 8, b, 128), BF),
            pltpu.VMEM((n, 2, 3, m, b, 128), BF),
            pltpu.VMEM((n, 2, m, b, 128), BF),
            pltpu.VMEM((n, 2, m, b, 128), F32),
            pltpu.VMEM((n, 2, 3, m, b // 4, 128), BF),
            pltpu.VMEM((n, 2, m, b // 4, 128), BF),
            pltpu.VMEM((n, 2, m, b // 4, 128), F32),
            pltpu.VMEM((n, 2, 3, m, b // 4, 128), BF),
            pltpu.VMEM((n, 2, 8, b, 128), BF),
        ]

    return pl.pallas_call(
        kernel,
        out_shape=jax.ShapeDtypeStruct((2048, 128), BF),
        in_specs=[any_] * 8,
        out_specs=any_,
        scratch_shapes=[
            pltpu.VMEM((2, 2048, 512), BF),
            pltpu.VMEM((2, 1024, 512), BF),
            pltpu.VMEM((2, 2048, 128), BF),
            pltpu.VMEM((2, 128, 2048), BF),
            pltpu.VMEM((2, 128, 1024), BF),
            pltpu.VMEM((1024, 128), BF),
            pltpu.VMEM((1024, 128), BF),
            pltpu.VMEM((2, 1024, 128), BF),
            pltpu.VMEM((1024, 256), F32),
            pltpu.VMEM((512, 128), F32),
            pltpu.VMEM((2, 4, 2, 4, 16, 1536), BF),
            pltpu.VMEM((2, 256, 1536), BF),
            pltpu.VMEM((2, 2, 8, 1536), F32),
        ]
        + reduce_scratch(2, 1, 128)
        + reduce_scratch(4, 2, 64)
        + [
            pltpu.SemaphoreType.DMA((N_SENT,)),
            pltpu.SemaphoreType.DMA((N_SEM,)),
            pltpu.SemaphoreType.DMA((10,)),
            pltpu.SMEM((4,), F32),
            pltpu.VMEM((1, 512), F32),
            pltpu.SMEM((1,), F32),
        ],
        compiler_params=pltpu.CompilerParams(
            collective_id=0, has_side_effects=True, vmem_limit_bytes=56 * 2**20
        ),
    )(amplitudes, coulomb, df_factors, thc_left, thc_right, occ, vir.reshape(1, 512), pivot)


def solution(mesh):
    in_specs = (
        P("pair", "aux"),
        P("pair", None),
        P("pair", "aux"),
        P("pair", "aux"),
        P("pair", "aux"),
        P("pair"),
        P(),
        P(),
    )
    return jax.shard_map(
        per_device, mesh=mesh, in_specs=in_specs, out_specs=P("pair", "aux"), check_vma=False
    )
```
